32 devices in a mesh: fx: 4 (over y, x), fy: 8 (over z, core).
Axes of the slice: x: 2, y: 2, z: 4, core: 2. Of those that a mesh axis runs over, the one named last changes fastest.
Arguments:
- sky: bfloat16 [4096, 32768], P('fx', 'fy'), may hold values from -6 to 6
- sub_off: int32 [2, 4], replicated, may hold values from 0 to 32767
- readers: int32 [32], replicated, may hold values from 0 to 3, as said below
- vis_cells: int32 [2, 65536], P(None, ('fx', 'fy')), may hold values from 0 to 504
- row_kernel: bfloat16 [8, 65536], P(None, ('fx', 'fy')), may hold values from 0.049804688 to 1
- col_kernel: float32 [8, 65536], P(None, ('fx', 'fy')), may hold values from 0.05 to 1
Outputs:
- vis: float32 [2, 65536], P(None, ('fx', 'fy'))
The draws below stay inside these ranges and needn't reach their ends.
Inputs may be any that keep to these rules, and one draw needn't show every extreme that they name: `readers`: every subgrid is read by at least one reader.
All inputs are finite; a program needn't handle non-finite values.
Results may differ from the reference program's by a relative error of at most 0.0064.
Values may be sent and summed in bfloat16 or wider, within the bound.
No kernel may reach another device: no remote copies, remote signals or barrier semaphores. Data moves between devices by JAX's collectives and lax.ppermute only.
A program may use at most 128 MiB of HBM per device.

```python
import math
import jax
import jax.numpy as jnp
from jax import lax

FACET = 4096
SUB = 512
K = 128
W = 8
FR = 512
NSUB = 4
NV = 2048
FACETS_X = 8
FACETS_Y = 8
SKY = 32768
READERS = 32
ROWS = 4096
VIS = 65536


def draw_readers(key, part):
    first_key, second_key, third_key = jax.random.split(key, 3)
    extra = READERS - NSUB
    first_pick = jax.random.randint(first_key, (extra,), 0, NSUB, dtype=jnp.int32)
    second_pick = jax.random.randint(second_key, (extra,), 0, NSUB, dtype=jnp.int32)
    listed = jnp.concatenate([jnp.arange(NSUB, dtype=jnp.int32), jnp.minimum(first_pick, second_pick)])
    return jax.random.permutation(third_key, listed)


def with_ends(drawn, own_key, least, largest):
    shape = drawn.shape
    place = [jax.random.randint(jax.random.fold_in(own_key, axis), (), 0, shape[axis]) for axis in range(len(shape))]
    drawn = drawn.at[tuple(place)].set(least)
    longest = shape.index(max(shape))
    place[longest] = (place[longest] + 1) % shape[longest]
    return drawn.at[tuple(place)].set(largest)


def shard_levels(rng, dims, shards, least, high):
    loudness, own = 1.0, jax.random.fold_in(rng, 6)
    for axis_at, shards_of in shards:
        heights = jnp.exp(jax.random.uniform(jax.random.fold_in(own, axis_at), (shards_of,), jnp.float32, least / len(shards), high / len(shards)))
        loudness = loudness * jnp.repeat(heights, dims[axis_at] // shards_of).reshape([-1 if axis == axis_at else 1 for axis in range(len(dims))])
    return loudness


def noise(own_key, dims, scale, limit, pieces=(), kind=jnp.bfloat16):
    loudness = shard_levels(own_key, dims, pieces, -0.22, 0.18) if pieces else 1.0
    entries = jax.random.normal(own_key, dims, jnp.float32) * scale * loudness
    return jnp.minimum(jnp.maximum(entries, -limit), limit).astype(kind)


def setup_inputs(seed: int = 0) -> dict:
    key_list = jax.random.split(jax.random.key(seed), 7)
    return {
        "sky": noise(key_list[0], (ROWS, SKY), 1.0, 6.0, ((0, 4), (1, 8))),
        "sub_off": with_ends(jax.random.randint(key_list[1], (2, NSUB), 0, SKY), jax.random.fold_in(key_list[1], 1), 0, SKY - 1).astype(jnp.int32),
        "readers": draw_readers(jax.random.fold_in(key_list[6], 71), 0),
        "vis_cells": with_ends(jax.random.randint(key_list[3], (2, VIS), 0, SUB - W + 1), jax.random.fold_in(key_list[3], 1), 0, SUB - W).astype(jnp.int32),
        "row_kernel": jnp.clip(jnp.exp(math.log(1.0) - 2.9996462 * jax.random.uniform(key_list[4], (W, VIS), jnp.float32) ** shard_levels(key_list[4], (W, VIS), ((1, 32),), -0.2, 0.2)), 0.049804688, 1.0).astype(jnp.bfloat16),
        "col_kernel": jnp.clip(jnp.exp(math.log(1.0) - 2.9957323 * jax.random.uniform(key_list[5], (W, VIS), jnp.float32) ** shard_levels(key_list[5], (W, VIS), ((1, 32),), -0.2, 0.2)), 0.05, 1.0),
    }


def phase_mod(upper, lower, sky_cells):
    return (upper % 256 * lower + upper // 256 * lower % sky_cells * 256) % sky_cells

def unit_angle(phase, sky_cells):
    return phase.astype(jnp.float32) * (2.0 * math.pi / sky_cells)

def resample_table(start, sky_cells):
    tap_index = jnp.arange(K, dtype=jnp.int32)
    grid_cells = jnp.arange(SUB, dtype=jnp.int32)
    places = (start + tap_index * (sky_cells // SUB)) % sky_cells
    forward = unit_angle(phase_mod(grid_cells[:, None], places[None, :], sky_cells), sky_cells)
    backward = -unit_angle(phase_mod(SUB // K * tap_index[None, :], places[:, None], sky_cells), sky_cells)
    wave_real, wave_imag = (jnp.cos(forward), jnp.sin(forward))
    back_real, back_imag = (jnp.cos(backward) / K, jnp.sin(backward) / K)
    highest = lax.Precision.HIGHEST
    real_part = jnp.dot(wave_real, back_real, precision=highest) - jnp.dot(wave_imag, back_imag, precision=highest)
    imag_part = jnp.dot(wave_real, back_imag, precision=highest) + jnp.dot(wave_imag, back_real, precision=highest)
    return (real_part, imag_part)

def row_stack(real_part, imag_part):
    return jnp.stack([jnp.stack([real_part, -imag_part], 1), jnp.stack([imag_part, real_part], 1)], 1).astype(jnp.bfloat16)

def col_stack(real_part, imag_part, factor):
    return jnp.stack([jnp.stack([real_part, imag_part]), jnp.stack([-imag_part, real_part])]) * factor

def strip_table(col_offsets, col_start, sky_cells):
    columns = col_start + jnp.arange(FACET, dtype=jnp.int32)
    frequency = col_offsets[:, None] + SUB // K * jnp.arange(K, dtype=jnp.int32)[None, :]
    angles = -unit_angle(phase_mod(frequency[None, :, :], columns[:, None, None], sky_cells), sky_cells)
    values_table = jnp.stack([jnp.cos(angles), jnp.sin(angles)], 2) / math.sqrt(FACET)
    return values_table.reshape(FACET, NSUB * 2 * K).astype(jnp.bfloat16)

def row_transform(row_offsets, row_start, sky_cells):
    rows_here = row_start + jnp.arange(FR, dtype=jnp.int32)
    frequency = row_offsets[:, None] + SUB // K * jnp.arange(K, dtype=jnp.int32)[None, :]
    angles = -unit_angle(phase_mod(frequency[:, :, None], rows_here[None, None, :], sky_cells), sky_cells)
    wave_real = jnp.cos(angles) / math.sqrt(FR)
    wave_imag = jnp.sin(angles) / math.sqrt(FR)
    real_rows = jnp.stack([wave_real, -wave_imag], 2)
    imag_rows = jnp.stack([wave_imag, wave_real], 2)
    return jnp.stack([real_rows, imag_rows], 1).astype(jnp.bfloat16)

def degridding(subgrid, vis_cells, row_kernel, col_kernel):
    grid_cells = jnp.arange(SUB, dtype=jnp.int32)
    row_gap = grid_cells[None, :] - vis_cells[0][:, None]
    col_gap = grid_cells[None, :] - vis_cells[1][:, None]
    row_weights = jnp.zeros(row_gap.shape, jnp.float32)
    col_weights = jnp.zeros(col_gap.shape, jnp.float32)
    for tap_index in range(row_kernel.shape[0]):
        row_weights = row_weights + jnp.where(row_gap == tap_index, row_kernel[tap_index].astype(jnp.float32)[:, None], 0.0)
        col_weights = col_weights + jnp.where(col_gap == tap_index, col_kernel[tap_index][:, None], 0.0)
    spread = jnp.dot(row_weights.astype(jnp.bfloat16), subgrid.reshape(SUB, 2 * SUB), preferred_element_type=jnp.float32)
    spread = spread.reshape(-1, 2, SUB)
    return lax.optimization_barrier(jnp.sum(spread * col_weights[:, None, :], axis=2)).T

def reference(sky, sub_off, readers, vis_cells, row_kernel, col_kernel):
    sky_cells = FACET * FACETS_Y
    row_spacing = sky_cells // FACETS_X
    factor = 1.0 / math.sqrt(FACETS_X * FACETS_Y)

    def column_turn(total, col_index):
        col_start = col_index * FACET
        values_table = strip_table(sub_off[1], col_start, sky_cells)

        def row_turn(summed, row_index):
            facet_block = lax.dynamic_slice(sky, (row_index * FR, col_start), (FR, FACET))
            strips = jnp.dot(facet_block, values_table, preferred_element_type=jnp.float32).astype(jnp.bfloat16)
            strips = strips.reshape(FR, NSUB, 2, K)
            row_start = row_index * row_spacing
            row_table = row_transform(sub_off[0], row_start, sky_cells)
            blocks = jnp.einsum('sqkpr,rspl->sqkl', row_table.astype(jnp.float32), strips.astype(jnp.float32)).astype(jnp.bfloat16)
            resampler = row_stack(*resample_table(row_start, sky_cells))
            update = jnp.einsum('mdqk,sqkl->mdsl', resampler.astype(jnp.float32), blocks.astype(jnp.float32))
            return (summed + update, None)
        summed, unused = lax.scan(row_turn, jnp.zeros((SUB, 2, NSUB, K), jnp.float32), jnp.arange(FACETS_X, dtype=jnp.int32))
        col_table = col_stack(*resample_table(col_start, sky_cells), factor)
        update = jnp.einsum('mcsl,cdnl->mdsn', summed, col_table, precision=lax.Precision.HIGHEST)
        return (total + update, None)
    total, unused = lax.scan(column_turn, jnp.zeros((SUB, 2, NSUB, SUB), jnp.float32), jnp.arange(FACETS_Y, dtype=jnp.int32))
    subgrids = total.astype(jnp.bfloat16)
    cells_by_reader = vis_cells.reshape(2, READERS, NV).transpose(1, 0, 2)
    rows_by_reader = row_kernel.reshape(W, READERS, NV).transpose(1, 0, 2)
    cols_by_reader = col_kernel.reshape(W, READERS, NV).transpose(1, 0, 2)

    def reader_turn(inputs):
        chosen, cells_here, rows_here, cols_here = inputs
        subgrid = lax.dynamic_index_in_dim(subgrids, chosen, 2, keepdims=False)
        return degridding(subgrid, cells_here, rows_here, cols_here)
    results = lax.map(reader_turn, (readers, cells_by_reader, rows_by_reader, cols_by_reader))
    return results.transpose(1, 0, 2).reshape(2, VIS)
```

```python
import functools
import math

import jax
import jax.numpy as jnp
from jax import lax
from jax.experimental import pallas as pl
from jax.experimental.pallas import tpu as pltpu
from jax.sharding import PartitionSpec as P

FACET = 4096
SUB = 512
K = 128
FR = 512
NSUB = 4
W = 8
STEP = 64
KBLOCK = 512
VBLOCK = 256
HALF = SUB // 2
F32 = jnp.float32
BF16 = jnp.bfloat16


def phase_mod(upper, lower, sky_cells):
    return (upper % 256 * lower + upper // 256 * lower % sky_cells * 256) % sky_cells


def wave(phase, period):
    quarter = (phase * 4 + period // 2) // period
    theta = (phase - quarter * (period // 4)).astype(F32) * (2.0 * math.pi / period)
    square = theta * theta
    sine = theta * (
        1.0
        + square
        * (-1.0 / 6 + square * (1.0 / 120 + square * (-1.0 / 5040 + square * (1.0 / 362880))))
    )
    cosine = 1.0 + square * (
        -0.5
        + square
        * (1.0 / 24 + square * (-1.0 / 720 + square * (1.0 / 40320 - square * (1.0 / 3628800))))
    )
    odd = quarter % 2 == 1
    real_part = jnp.where(odd, sine, cosine)
    imag_part = jnp.where(odd, cosine, sine)
    real_part = jnp.where((quarter == 1) | (quarter == 2), -real_part, real_part)
    imag_part = jnp.where((quarter == 2) | (quarter == 3), -imag_part, imag_part)
    return real_part, imag_part


def turn(upper, lower, sky_cells):
    real_part, imag_part = wave(phase_mod(upper, lower, sky_cells), sky_cells)
    return real_part, -imag_part


def amplitude(gap):
    top = wave(gap % (2 * SUB // K), 2 * SUB // K)[1]
    below = wave(gap % (2 * SUB), 2 * SUB)[1]
    return jnp.where(gap == 0, 1.0, top / (K * jnp.where(gap == 0, 1.0, below)))


def resample(start, cells, sky_cells):
    taps = SUB // K * jnp.arange(K, dtype=jnp.int32)
    middle = ((K - 1) * (sky_cells // (2 * SUB)) + start) % sky_cells
    cell_real, cell_imag = wave(phase_mod(cells[None, :], middle[:, None], sky_cells), sky_cells)
    tap_real, tap_imag = turn(taps[None, :], middle[:, None], sky_cells)
    size = amplitude(cells[:, None] - taps[None, :])[None]
    cell_real, cell_imag = cell_real[:, :, None], cell_imag[:, :, None]
    tap_real, tap_imag = tap_real[:, None, :], tap_imag[:, None, :]
    return (
        size * (cell_real * tap_real - cell_imag * tap_imag),
        size * (cell_real * tap_imag + cell_imag * tap_real),
    )


def expand(coarse_real, coarse_imag, fine_real, fine_imag):
    return (
        coarse_real * fine_real - coarse_imag * fine_imag,
        coarse_real * fine_imag + coarse_imag * fine_real,
    )


def blocks_kernel(count, facets, coarse_col, fine_col, coarse_row, fine_row, sky, out, total, table):
    step = pl.program_id(0)
    steps = pl.num_programs(0)
    pieces = table.shape[0] // STEP
    coarse = coarse_col[pl.ds(pl.multiple_of(step * pieces, pieces), pieces), :]
    for s in range(count):
        re, im = slice(2 * s * K, (2 * s + 1) * K), slice((2 * s + 1) * K, (2 * s + 2) * K)
        fine_real, fine_imag = fine_col[:, re], fine_col[:, im]
        for piece in range(pieces):
            row = slice(piece, piece + 1)
            real_part, imag_part = expand(coarse[row, re], coarse[row, im], fine_real, fine_imag)
            table[piece * STEP : (piece + 1) * STEP, re] = real_part.astype(BF16)
            table[piece * STEP : (piece + 1) * STEP, im] = imag_part.astype(BF16)
    update = jnp.dot(sky[...], table[...], preferred_element_type=F32)

    @pl.when(step == 0)
    def _():
        total[...] = update

    @pl.when(step > 0)
    def _():
        total[...] += update

    @pl.when(step == steps - 1)
    def _():
        for s in range(count):
            re, im = slice(2 * s * K, (2 * s + 1) * K), slice((2 * s + 1) * K, (2 * s + 2) * K)
            for a in range(facets):
                strips = total[a * FR : (a + 1) * FR, 2 * s * K : (2 * s + 2) * K].astype(BF16)
                rows = []
                for piece in range(FR // STEP):
                    row = slice(a * (FR // STEP) + piece, a * (FR // STEP) + piece + 1)
                    rows.append(
                        jnp.concatenate(
                            expand(
                                coarse_row[row, re], coarse_row[row, im], fine_row[:, re], fine_row[:, im]
                            ),
                            axis=1,
                        )
                    )
                turned = jnp.concatenate(rows, axis=0).astype(BF16)
                product = lax.dot_general(
                    strips, turned, (((0,), (0,)), ((), ())), preferred_element_type=F32
                )
                real_part = product[:K, :K] - product[K:, K:]
                imag_part = product[:K, K:] + product[K:, :K]
                out[s, :, 2 * a * K : (2 * a + 1) * K] = real_part.astype(BF16)
                out[s, :, (2 * a + 1) * K : (2 * a + 2) * K] = imag_part.astype(BF16)


def facet_blocks(sky, tables):
    rows, columns = sky.shape
    count = tables[0].shape[1] // (2 * K)
    facets = rows // FR
    whole = lambda array: pl.BlockSpec(array.shape, lambda step: (0,) * array.ndim)
    return pl.pallas_call(
        functools.partial(blocks_kernel, count, facets),
        grid=(columns // KBLOCK,),
        in_specs=[whole(table) for table in tables]
        + [pl.BlockSpec((rows, KBLOCK), lambda step: (0, step))],
        out_specs=pl.BlockSpec((count, K, 2 * facets * K), lambda step: (0, 0, 0)),
        out_shape=jax.ShapeDtypeStruct((count, K, 2 * facets * K), BF16),
        scratch_shapes=[
            pltpu.VMEM((rows, 2 * K * count), F32),
            pltpu.VMEM((KBLOCK, 2 * K * count), BF16),
        ],
        cost_estimate=pl.CostEstimate(
            flops=4 * rows * columns * K * count, bytes_accessed=2 * rows * columns, transcendentals=0
        ),
        name="facet_blocks",
    )(*tables, sky)


def columns_kernel(count, facets, table, *refs):
    blocks, out = refs[:count], refs[count]
    total = None
    for pair in range(0, count, 2):
        stacked = jnp.concatenate([block[...] for block in blocks[pair : pair + 2]], axis=0)
        part = jnp.dot(
            table[:, pair * K : pair * K + stacked.shape[0]], stacked, preferred_element_type=F32
        )
        total = part if total is None else total + part
    for a in range(facets):
        re, im = slice(2 * a * K, (2 * a + 1) * K), slice((2 * a + 1) * K, (2 * a + 2) * K)
        out[:HALF, a * K : (a + 1) * K] = (total[:HALF, re] - total[HALF:, im]).astype(BF16)
        out[HALF:, a * K : (a + 1) * K] = (total[:HALF, im] + total[HALF:, re]).astype(BF16)


def column_sums(table, blocks):
    facets = blocks[0].shape[1] // (2 * K)
    return pl.pallas_call(
        functools.partial(columns_kernel, len(blocks), facets),
        out_shape=jax.ShapeDtypeStruct((2 * HALF, facets * K), BF16),
        cost_estimate=pl.CostEstimate(
            flops=4 * HALF * table.shape[1] * 2 * facets * K, bytes_accessed=1 << 21, transcendentals=0
        ),
        name="column_sums",
    )(table, *blocks)


def taps_of(first, kernel, shape):
    row = lax.broadcasted_iota(jnp.int32, shape, 0)
    tap = (row - first) & (W - 1)
    value = jnp.zeros(shape, F32)
    for e in range(W):
        value = jnp.where(tap == e, kernel[e : e + 1, :], value)
    return value, (first - row + (W - 1)) >> 3


def degrid_kernel(count, active, first, table, queries, *refs):
    sums, out, subgrid = refs[:count], refs[count], refs[count + 1]
    total = None
    width = sums[0].shape[1]
    for source in range(count):
        part = jnp.dot(
            sums[source][...],
            table[source * width : (source + 1) * width, :],
            preferred_element_type=F32,
        )
        total = part if total is None else total + part
    subgrid[:HALF, :] = (total[:HALF, :SUB] - total[HALF:, SUB:]).astype(BF16)
    subgrid[HALF:, :] = (total[:HALF, SUB:] + total[HALF:, :SUB]).astype(BF16)
    slots, _, visibilities = queries.shape

    def slot_turn(slot, carry):
        @pl.when(active[slot] == 0)
        def _():
            out[slot] = jnp.zeros(out.shape[1:], F32)

        @pl.when(active[slot] != 0)
        def _():
            def block_turn(block, carry):
                here = pl.ds(pl.multiple_of(block * VBLOCK, VBLOCK), VBLOCK)
                rows = queries[slot, :, here].astype(F32)
                u = (rows[16:17] * 2.0 + rows[17:18]).astype(jnp.int32)
                w = (rows[18:19] * 2.0 + rows[19:20]).astype(jnp.int32)
                row_value, row_group = taps_of(u, rows[0:8], (W, VBLOCK))
                groups = lax.broadcasted_iota(jnp.int32, (SUB // W, W, VBLOCK), 0)
                weights = jnp.where(groups == row_group[None], row_value[None], 0.0)
                weights = weights.reshape(SUB, VBLOCK).astype(BF16)
                spread = jnp.dot(subgrid[...], weights, preferred_element_type=F32)
                spread = spread.reshape(2, HALF // W, W, VBLOCK)
                col_value, col_group = taps_of(w, rows[8:16], (W, VBLOCK))
                groups = lax.broadcasted_iota(jnp.int32, (HALF // W, W, VBLOCK), 0)
                hit = groups == (col_group - first[0])[None]
                for p in range(2):
                    picked = jnp.sum(jnp.where(hit, spread[p], 0.0), axis=0)
                    out[slot, p : p + 1, here] = jnp.sum(picked * col_value, axis=0, keepdims=True)
                return carry

            lax.fori_loop(0, visibilities // VBLOCK, block_turn, 0)

        return carry

    lax.fori_loop(0, slots, slot_turn, 0)


def degrid(active, first, table, queries, sums):
    slots, _, visibilities = queries.shape
    smem = pl.BlockSpec(memory_space=pltpu.SMEM)
    vmem = pl.BlockSpec(memory_space=pltpu.VMEM)
    return pl.pallas_call(
        functools.partial(degrid_kernel, len(sums)),
        in_specs=[smem, smem] + [vmem] * (2 + len(sums)),
        out_specs=vmem,
        out_shape=jax.ShapeDtypeStruct((slots, 2, visibilities), F32),
        scratch_shapes=[pltpu.VMEM((2 * HALF, SUB), BF16)],
        cost_estimate=pl.CostEstimate(flops=1 << 33, bytes_accessed=1 << 22, transcendentals=0),
        name="degrid",
    )(active, first, table, queries, *sums)


def local(sky, sub_off, readers, vis_cells, row_kernel, col_kernel):
    rows_axis = lax.axis_size("fx")
    cols_axis = lax.axis_size("fy")
    planes = cols_axis // 2
    copies = planes // NSUB
    assert planes == copies * NSUB
    facets = sky.shape[0] // FR
    sky_cells = FACET * cols_axis
    facet_rows = facets * rows_axis
    row_spacing = sky_cells // facet_rows
    factor = 1.0 / math.sqrt(facet_rows * cols_axis)
    at_x, at_y = lax.axis_index("fx"), lax.axis_index("fy")
    plane, core = at_y // 2, at_y % 2
    own = plane // copies
    iota = functools.partial(jnp.arange, dtype=jnp.int32)

    def plane_shift(group_step, copy_step):
        moved = []
        for z in range(planes):
            to = (z // copies + group_step) % NSUB * copies + (z % copies + copy_step) % copies
            moved += [(2 * z + c, 2 * to + c) for c in range(2)]
        return moved

    swap = [(i, i ^ 1) for i in range(cols_axis)]

    steps = sorted(range(1, NSUB), key=lambda step: -min(step, NSUB - step)) + [0]
    order = (own + jnp.array(steps, dtype=jnp.int32)) % NSUB
    chosen = jnp.sum(
        jnp.where(order[None, :, None] == iota(NSUB)[None, None, :], sub_off[:, None, :], 0), axis=2
    )
    frequency = chosen[:, :, None] + SUB // K * iota(K)[None, None, :]

    def lanes(parts, scale):
        packed = jnp.stack(parts, axis=-2) * scale
        return packed.reshape(-1, NSUB * 2 * K)

    col_start = at_y * FACET
    coarse_at = col_start + STEP * iota(FACET // STEP)
    coarse_col = lanes(
        turn(frequency[1][None], coarse_at[:, None, None], sky_cells), 1.0 / math.sqrt(FACET)
    )
    fine_col = lanes(turn(frequency[1][None], iota(STEP)[:, None, None], sky_cells), 1.0)
    row_starts = (at_x * facets + iota(facets)) * row_spacing
    coarse_at = (row_starts[:, None] + STEP * iota(FR // STEP)[None, :]).reshape(-1)
    coarse_row = lanes(
        turn(frequency[0][None], coarse_at[:, None, None], sky_cells), 1.0 / math.sqrt(FR)
    )
    fine_row = lanes(turn(frequency[0][None], iota(STEP)[:, None, None], sky_cells), 1.0)
    tables = (coarse_col, fine_col, coarse_row, fine_row)

    def blocks_of(start, count):
        return facet_blocks(
            sky, tuple(table[:, 2 * K * start : 2 * K * (start + count)] for table in tables)
        )

    blocks, sources = [], []
    for start in range(0, NSUB, 2):
        pair = blocks_of(start, 2)
        for at in range(2):
            for copy_step in range(copies):
                step = steps[start + at]
                moved = pair[at]
                if step or copy_step:
                    moved = lax.ppermute(moved, "fy", plane_shift(step, copy_step))
                blocks.append(moved)
                sources.append((own - step) % NSUB * copies + (plane - copy_step) % copies)
    blocks += [lax.ppermute(block, "fy", swap) for block in blocks]
    source_planes = jnp.stack(sources)

    starts = jnp.concatenate([2 * source_planes + core, 2 * source_planes + 1 - core]) * FACET
    cells = core * HALF + iota(HALF)
    col_table = jnp.stack(resample(starts, cells, sky_cells)) * factor
    col_table = col_table.transpose(0, 2, 1, 3).reshape(2 * HALF, -1).astype(BF16)
    sums = [column_sums(col_table, blocks)]

    rows_of = [at_x]
    for step in range(1, rows_axis):
        ring = [(i, (i + step) % rows_axis) for i in range(rows_axis)]
        sums.append(lax.ppermute(sums[0], "fx", ring))
        rows_of.append((at_x - step) % rows_axis)
    facet_at = (jnp.stack(rows_of)[:, None] * facets + iota(facets)[None, :]).reshape(-1)
    row_table = jnp.stack(resample(facet_at * row_spacing, iota(SUB), sky_cells))
    row_table = row_table.transpose(1, 3, 0, 2).reshape(-1, 2 * SUB).astype(BF16)

    cells_high, cells_low = vis_cells // 2, vis_cells % 2
    query = jnp.concatenate(
        [
            row_kernel,
            col_kernel.astype(BF16),
            jnp.stack([cells_high[0], cells_low[0], cells_high[1], cells_low[1]]).astype(BF16),
        ]
    )
    queries, readers_of = [query], [plane]
    for step in range(1, planes):
        ring = [(i, (i + 2 * step) % cols_axis) for i in range(cols_axis)]
        queries.append(lax.ppermute(query, "fy", ring))
        readers_of.append((plane - step) % planes)
    queries = jnp.stack(queries)
    queries = jnp.concatenate([queries, lax.ppermute(queries, "fy", swap)])
    reader_plane = jnp.stack(readers_of)
    reader_at = at_x * cols_axis + 2 * reader_plane
    reader_at = jnp.concatenate([reader_at + core, reader_at + 1 - core])
    wanted = jnp.sum(
        jnp.where(reader_at[:, None] == iota(readers.shape[0])[None, :], readers[None, :], 0), axis=1
    )
    mine = jnp.concatenate([reader_plane, reader_plane]) % copies == plane % copies
    active = ((wanted == own) & mine).astype(jnp.int32)
    first = (core * (HALF // W)).astype(jnp.int32).reshape(1)

    results = degrid(active, first, row_table, queries, sums)

    both = results[:planes] + lax.ppermute(results[planes:], "fy", swap)
    vis = both[0]
    for step in range(1, planes):
        ring = [(i, (i - 2 * step) % cols_axis) for i in range(cols_axis)]
        vis = vis + lax.ppermute(both[step], "fy", ring)
    return vis


def solution(mesh):
    return jax.shard_map(
        local,
        mesh=mesh,
        in_specs=(
            P("fx", "fy"),
            P(),
            P(),
            P(None, ("fx", "fy")),
            P(None, ("fx", "fy")),
            P(None, ("fx", "fy")),
        ),
        out_specs=P(None, ("fx", "fy")),
        check_vma=False,
    )
```

```python
import functools
import math

import jax
import jax.numpy as jnp
from jax import lax
from jax.experimental import pallas as pl
from jax.experimental.pallas import tpu as pltpu
from jax.sharding import PartitionSpec as P


FACET = 4096
SUB = 512
K = 128
FR = 512
NSUB = 4
W = 8
STEP = 64
GROUP = 8
VBLOCK = 256
HALF = SUB // 2
F32 = jnp.float32
BF16 = jnp.bfloat16
SMEM = pl.BlockSpec(memory_space=pltpu.SMEM)
VMEM = pl.BlockSpec(memory_space=pltpu.VMEM)
ANY = pl.BlockSpec(memory_space=pl.ANY)


def wave(turns, period):
    bits = period.bit_length() - 1
    phase = turns & (period - 1)
    quarter = (phase + period // 8) >> (bits - 2)
    theta = (phase - (quarter << (bits - 2))).astype(F32) * (2.0 * math.pi / period)
    square = theta * theta
    sine = theta * (
        1.0
        + square
        * (-1.0 / 6 + square * (1.0 / 120 + square * (-1.0 / 5040 + square * (1.0 / 362880))))
    )
    cosine = 1.0 + square * (
        -0.5
        + square
        * (1.0 / 24 + square * (-1.0 / 720 + square * (1.0 / 40320 - square * (1.0 / 3628800))))
    )
    odd = (quarter & 1) == 1
    real_part = jnp.where(odd, sine, cosine)
    imag_part = jnp.where(odd, cosine, sine)
    real_part = jnp.where(((quarter + 1) & 2) == 2, -real_part, real_part)
    imag_part = jnp.where((quarter & 2) == 2, -imag_part, imag_part)
    return real_part, imag_part


def turn(first, second, sky_cells, scale=1.0):
    real_part, imag_part = wave(first * second, sky_cells)
    return real_part * scale, imag_part * -scale


def amplitude(gap):
    top = wave(gap, 2 * SUB // K)[1]
    below = wave(gap, 2 * SUB)[1]
    return jnp.where(gap == 0, 1.0, top / (K * jnp.where(gap == 0, 1.0, below)))


def middle_of(start, sky_cells):
    return start + (K - 1) * (sky_cells // (2 * SUB))


def iota(shape, dimension):
    return lax.broadcasted_iota(jnp.int32, shape, dimension)


def expand(coarse_real, coarse_imag, fine_real, fine_imag):
    return (
        coarse_real * fine_real - coarse_imag * fine_imag,
        coarse_real * fine_imag + coarse_imag * fine_real,
    )


def parts_of(index):
    return slice(2 * index * K, (2 * index + 1) * K), slice((2 * index + 1) * K, (2 * index + 2) * K)


def tables_kernel(steps, geometry, meta, out_cols, out_rows, coarse_col, fine_col):
    sky_cells, row_spacing, copies = geometry
    count, columns = len(steps), out_cols.shape[1]
    facets = out_rows.shape[0] // count
    at_x, at_y = meta[0], meta[1]
    own = at_y // 2 // copies
    lane, row = iota((STEP, K), 1), iota((STEP, K), 0)
    re, im = parts_of(0)
    for s, step in enumerate(steps):
        chosen = (own + step) % NSUB
        pair, (out_re, out_im) = s // 2, parts_of(s % 2)
        frequency = meta[2 + NSUB + chosen] + SUB // K * lane
        coarse_col[s, :, re], coarse_col[s, :, im] = turn(
            frequency, at_y * FACET + STEP * row, sky_cells, 1.0 / math.sqrt(FACET)
        )
        fine_col[:, re], fine_col[:, im] = turn(frequency, row, sky_cells)

        def table_turn(group, carry):
            coarse = coarse_col[s, pl.ds(pl.multiple_of(group * GROUP, GROUP), GROUP), :]
            for piece in range(GROUP):
                here = pl.ds(pl.multiple_of((group * GROUP + piece) * STEP, STEP), STEP)
                real_part, imag_part = expand(
                    coarse[piece : piece + 1, re],
                    coarse[piece : piece + 1, im],
                    fine_col[:, re],
                    fine_col[:, im],
                )
                out_cols[pair, here, out_re] = real_part.astype(BF16)
                out_cols[pair, here, out_im] = imag_part.astype(BF16)
            return carry

        lax.fori_loop(0, columns // (STEP * GROUP), table_turn, 0)
        frequency = meta[2 + chosen] + SUB // K * lane
        fine_real, fine_imag = turn(frequency, row, sky_cells)
        pieces = FR // STEP
        for a in range(facets):
            row_start = (at_x * facets + a) * row_spacing
            coarse_real, coarse_imag = turn(
                frequency[:pieces], row_start + STEP * row[:pieces], sky_cells, 1.0 / math.sqrt(FR)
            )
            for piece in range(pieces):
                here = slice(piece * STEP, (piece + 1) * STEP)
                real_part, imag_part = expand(
                    coarse_real[piece : piece + 1],
                    coarse_imag[piece : piece + 1],
                    fine_real,
                    fine_imag,
                )
                out_rows[s * facets + a, here, re] = real_part.astype(BF16)
                out_rows[s * facets + a, here, im] = imag_part.astype(BF16)


def strip_tables(meta, sky, steps, geometry):
    count, (rows, columns) = len(steps), sky.shape
    facets = rows // FR
    return pl.pallas_call(
        functools.partial(tables_kernel, steps, geometry),
        in_specs=[SMEM],
        out_specs=[VMEM] * 2,
        out_shape=[
            jax.ShapeDtypeStruct((count // 2, columns, 4 * K), BF16),
            jax.ShapeDtypeStruct((count * facets, FR, 2 * K), BF16),
        ],
        scratch_shapes=[
            pltpu.VMEM((count, columns // STEP, 2 * K), F32),
            pltpu.VMEM((STEP, 2 * K), F32),
        ],
        cost_estimate=pl.CostEstimate(flops=1 << 33, bytes_accessed=1 << 24, transcendentals=0),
        compiler_params=pltpu.CompilerParams(vmem_limit_bytes=16 << 20),
        name="strip_tables",
    )(meta)


def blocks_kernel(pair, sky, cols, rows, *outs):
    facets = sky.shape[0] // FR
    for a in range(facets):
        strips = jnp.dot(
            sky[a * FR : (a + 1) * FR, :], cols[pair], preferred_element_type=F32
        ).astype(BF16)
        for s in range(2):
            product = lax.dot_general(
                strips[:, 2 * s * K : (2 * s + 2) * K],
                rows[(2 * pair + s) * facets + a],
                (((0,), (0,)), ((), ())),
                preferred_element_type=F32,
            )
            re, im = parts_of(a)
            outs[s][:, re] = (product[:K, :K] - product[K:, K:]).astype(BF16)
            outs[s][:, im] = (product[:K, K:] + product[K:, :K]).astype(BF16)


def facet_blocks(sky, tables, pair):
    rows, columns = sky.shape
    facets = rows // FR
    return pl.pallas_call(
        functools.partial(blocks_kernel, pair),
        in_specs=[VMEM] * 3,
        out_specs=[VMEM] * 2,
        out_shape=[jax.ShapeDtypeStruct((K, 2 * facets * K), BF16)] * 2,
        cost_estimate=pl.CostEstimate(
            flops=8 * rows * columns * K, bytes_accessed=2 * rows * columns, transcendentals=0
        ),
        compiler_params=pltpu.CompilerParams(vmem_limit_bytes=28 << 20),
        name="facet_blocks",
    )(sky, *tables)


def col_table_kernel(geometry, factor, place, after, out):
    sky_cells, copies, sources = geometry
    planes = len(sources) * copies
    period = 2 * planes
    at_y = place[1]
    plane, core = at_y // 2, at_y % 2
    own = plane // copies
    gap = core * HALF + iota((HALF, K), 0) - SUB // K * iota((HALF, K), 1)
    size = amplitude(gap) * factor
    real_part, imag_part = wave(gap * middle_of(0, sky_cells), sky_cells)
    folded = (HALF // period, period, K)
    real_part = (size * real_part).reshape(folded)
    imag_part = (size * imag_part).reshape(folded)
    steps = gap[:period]
    at = 0
    for other in range(2):
        for step in sources:
            for copy_step in range(copies):
                source = (own + NSUB - step) % NSUB * copies + (plane + copies - copy_step) % copies
                turned = wave(steps * (2 * source + (core + other) % 2), period)
                both = expand(real_part, imag_part, turned[0][None], turned[1][None])
                out[at, :HALF, :] = both[0].reshape(HALF, K).astype(BF16)
                out[at, HALF:, :] = both[1].reshape(HALF, K).astype(BF16)
                at += 1


def row_table_kernel(geometry, place, after, out):
    sky_cells, facets, rows_axis = geometry
    period = facets * rows_axis
    gap = iota((K, SUB), 1) - SUB // K * iota((K, SUB), 0)
    size = amplitude(gap)
    real_part, imag_part = wave(gap * middle_of(0, sky_cells), sky_cells)
    folded = (K // period, period, SUB)
    real_part = (size * real_part).reshape(folded)
    imag_part = (size * imag_part).reshape(folded)
    steps = gap[:period]
    for source in range(period):
        step, a = source // facets, source % facets
        facet_row = (place[0] + rows_axis - step) % rows_axis * facets + a
        turned = wave(steps * facet_row, period)
        both = expand(real_part, imag_part, turned[0][None], turned[1][None])
        out[source, :, :SUB] = both[0].reshape(K, SUB).astype(BF16)
        out[source, :, SUB:] = both[1].reshape(K, SUB).astype(BF16)


def columns_kernel(count, facets, table, *refs):
    blocks, out = refs[:count], refs[count]
    total = None
    for pair in range(0, count, 2):
        stacked = jnp.concatenate([block[...] for block in blocks[pair : pair + 2]], axis=0)
        turned = jnp.concatenate([table[at] for at in range(pair, min(pair + 2, count))], axis=1)
        part = jnp.dot(turned, stacked, preferred_element_type=F32)
        total = part if total is None else total + part
    for a in range(facets):
        re, im = parts_of(a)
        out[:HALF, a * K : (a + 1) * K] = (total[:HALF, re] - total[HALF:, im]).astype(BF16)
        out[HALF:, a * K : (a + 1) * K] = (total[:HALF, im] + total[HALF:, re]).astype(BF16)


def column_sums(table, blocks):
    facets = blocks[0].shape[1] // (2 * K)
    return pl.pallas_call(
        functools.partial(columns_kernel, len(blocks), facets),
        out_shape=jax.ShapeDtypeStruct((2 * HALF, facets * K), BF16),
        cost_estimate=pl.CostEstimate(
            flops=8 * HALF * len(blocks) * facets * K * K, bytes_accessed=1 << 21, transcendentals=0
        ),
        compiler_params=pltpu.CompilerParams(vmem_limit_bytes=20 << 20),
        name="column_sums",
    )(table, *blocks)


def taps_of(first, kernel, shape):
    row = iota(shape, 0)
    tap = (row - first) & (W - 1)
    value = jnp.zeros(shape, F32)
    for e in range(W):
        value = jnp.where(tap == e, kernel[e : e + 1, :], value)
    return value, (first - row + (W - 1)) >> 3


def query_kernel(vis_cells, row_kernel, col_kernel, after, out):
    out[0:W, :] = row_kernel[...]
    out[W : 2 * W, :] = col_kernel[...].astype(BF16)
    cells = vis_cells[...]
    halves = [cells >> 1, cells & 1]
    cells = jnp.concatenate([half[axis : axis + 1] for axis in range(2) for half in halves])
    out[2 * W :, :] = cells.astype(F32).astype(BF16)


def degrid_kernel(geometry, place, readers, table, queries_own, queries_other, *refs):
    cols_axis, copies, count = geometry
    sums, outs, subgrid = refs[:count], refs[count : count + 2], refs[count + 2]
    at_x, at_y = place[0], place[1]
    plane, core = at_y // 2, at_y % 2
    own = plane // copies
    total = None
    facets = sums[0].shape[1] // K
    for source in range(count):
        turned = jnp.concatenate(
            [table[at] for at in range(source * facets, (source + 1) * facets)], axis=0
        )
        part = jnp.dot(sums[source][...], turned, preferred_element_type=F32)
        total = part if total is None else total + part
    subgrid[:HALF, :] = (total[:HALF, :SUB] - total[HALF:, SUB:]).astype(BF16)
    subgrid[HALF:, :] = (total[:HALF, SUB:] + total[HALF:, :SUB]).astype(BF16)
    planes, _, visibilities = queries_own.shape
    for other, (queries, out) in enumerate(zip((queries_own, queries_other), outs)):

        def slot_turn(slot, carry):
            source = (plane + planes - slot) % planes
            reader = at_x * cols_axis + 2 * source + (core + other) % 2
            active = (readers[reader] == own) & (source % copies == plane % copies)

            @pl.when(jnp.logical_not(active))
            def _():
                out[slot] = jnp.zeros(out.shape[1:], F32)

            @pl.when(active)
            def _():
                def block_turn(block, carry):
                    here = pl.ds(pl.multiple_of(block * VBLOCK, VBLOCK), VBLOCK)
                    rows = queries[slot, :, here].astype(F32)
                    u = (rows[16:17] * 2.0 + rows[17:18]).astype(jnp.int32)
                    w = (rows[18:19] * 2.0 + rows[19:20]).astype(jnp.int32)
                    row_value, row_group = taps_of(u, rows[0:8], (W, VBLOCK))
                    groups = iota((SUB // W, W, VBLOCK), 0)
                    weights = jnp.where(groups == row_group[None], row_value[None], 0.0)
                    weights = weights.reshape(SUB, VBLOCK).astype(BF16)
                    spread = jnp.dot(subgrid[...], weights, preferred_element_type=F32)
                    spread = spread.reshape(2, HALF // W, W, VBLOCK)
                    col_value, col_group = taps_of(w, rows[8:16], (W, VBLOCK))
                    groups = iota((HALF // W, W, VBLOCK), 0)
                    hit = groups == (col_group - core * (HALF // W))[None]
                    for p in range(2):
                        picked = jnp.sum(jnp.where(hit, spread[p], 0.0), axis=0)
                        out[slot, p : p + 1, here] = jnp.sum(
                            picked * col_value, axis=0, keepdims=True
                        )
                    return carry

                lax.fori_loop(0, visibilities // VBLOCK, block_turn, 0)

            return carry

        lax.fori_loop(0, planes, slot_turn, 0)


def degrid(place, readers, table, queries, others, sums, geometry):
    planes, _, visibilities = queries.shape
    result = jax.ShapeDtypeStruct((planes, 2, visibilities), F32)
    return pl.pallas_call(
        functools.partial(degrid_kernel, geometry + (len(sums),)),
        in_specs=[SMEM, SMEM] + [VMEM] * (3 + len(sums)),
        out_specs=[VMEM, VMEM],
        out_shape=[result, result],
        scratch_shapes=[pltpu.VMEM((2 * HALF, SUB), BF16)],
        cost_estimate=pl.CostEstimate(flops=1 << 33, bytes_accessed=1 << 22, transcendentals=0),
        compiler_params=pltpu.CompilerParams(vmem_limit_bytes=20 << 20),
        name="degrid",
    )(place, readers, table, queries, others, *sums)


def local(sky, sub_off, readers, vis_cells, row_kernel, col_kernel):
    rows_axis = lax.axis_size("fx")
    cols_axis = lax.axis_size("fy")
    planes = cols_axis // 2
    copies = planes // NSUB
    facets = sky.shape[0] // FR
    sky_cells = FACET * cols_axis
    facet_rows = facets * rows_axis
    row_spacing = sky_cells // facet_rows
    factor = 1.0 / math.sqrt(facet_rows * cols_axis)
    assert planes == copies * NSUB and sky_cells & (sky_cells - 1) == 0
    place = jnp.stack([lax.axis_index("fx"), lax.axis_index("fy")]).astype(jnp.int32)
    meta = jnp.concatenate([place, sub_off.reshape(-1)])

    def plane_shift(group_step, copy_step):
        moved = []
        for z in range(planes):
            to = (z // copies + group_step) % NSUB * copies + (z % copies + copy_step) % copies
            moved += [(2 * z + c, 2 * to + c) for c in range(2)]
        return moved

    swap = [(i, i ^ 1) for i in range(cols_axis)]

    steps = sorted(range(1, NSUB), key=lambda step: -min(step, NSUB - step)) + [0]
    tables = strip_tables(meta, sky, steps, (sky_cells, row_spacing, copies))
    blocks = []
    for start in range(0, NSUB, 2):
        pair = facet_blocks(sky, tables, start // 2)
        for step, block in zip(steps[start : start + 2], pair):
            for copy_step in range(copies):
                moved = block
                if step or copy_step:
                    moved = lax.ppermute(block, "fy", plane_shift(step, copy_step))
                blocks.append(moved)
    col_table = pl.pallas_call(
        functools.partial(col_table_kernel, (sky_cells, copies, steps), factor),
        in_specs=[SMEM, ANY],
        out_specs=VMEM,
        out_shape=jax.ShapeDtypeStruct((2 * len(blocks), 2 * HALF, K), BF16),
        cost_estimate=pl.CostEstimate(flops=1 << 22, bytes_accessed=1 << 20, transcendentals=1 << 20),
        compiler_params=pltpu.CompilerParams(vmem_limit_bytes=20 << 20),
        name="col_table",
    )(place, pair[0])
    query = pl.pallas_call(
        query_kernel,
        in_specs=[VMEM, VMEM, VMEM, ANY],
        out_specs=VMEM,
        out_shape=jax.ShapeDtypeStruct((2 * W + 4, vis_cells.shape[1]), BF16),
        compiler_params=pltpu.CompilerParams(vmem_limit_bytes=20 << 20),
        name="query",
    )(vis_cells, row_kernel, col_kernel, pair[0])
    last = len(blocks) - copies - 1
    blocks[last], _ = lax.optimization_barrier((blocks[last], col_table))
    blocks += [lax.ppermute(block, "fy", swap) for block in blocks]
    sums = [column_sums(col_table, blocks)]

    for step in range(1, rows_axis):
        ring = [(i, (i + step) % rows_axis) for i in range(rows_axis)]
        sums.append(lax.ppermute(sums[0], "fx", ring))
    row_table = pl.pallas_call(
        functools.partial(row_table_kernel, (sky_cells, facets, rows_axis)),
        in_specs=[SMEM, ANY],
        out_specs=VMEM,
        out_shape=jax.ShapeDtypeStruct((facet_rows, K, 2 * SUB), BF16),
        cost_estimate=pl.CostEstimate(
            flops=1 << 23, bytes_accessed=1 << 21, transcendentals=1 << 21
        ),
        compiler_params=pltpu.CompilerParams(vmem_limit_bytes=20 << 20),
        name="row_table",
    )(place, sums[0])

    moved, _ = lax.optimization_barrier((query, sums[0]))
    queries = [query]
    for step in range(1, planes):
        ring = [(i, (i + 2 * step) % cols_axis) for i in range(cols_axis)]
        queries.append(lax.ppermute(moved, "fy", ring))
    queries = jnp.stack(queries)
    others = lax.ppermute(queries, "fy", swap)
    results, others = degrid(
        place, readers, row_table, queries, others, sums, (cols_axis, copies)
    )

    both = results + lax.ppermute(others, "fy", swap)
    vis = both[0]
    for step in range(1, planes):
        ring = [(i, (i - 2 * step) % cols_axis) for i in range(cols_axis)]
        vis = vis + lax.ppermute(both[step], "fy", ring)
    return vis


def solution(mesh):
    return jax.shard_map(
        local,
        mesh=mesh,
        in_specs=(
            P("fx", "fy"),
            P(),
            P(),
            P(None, ("fx", "fy")),
            P(None, ("fx", "fy")),
            P(None, ("fx", "fy")),
        ),
        out_specs=P(None, ("fx", "fy")),
        check_vma=False,
    )
```

```python
import functools
import math

import jax
import jax.numpy as jnp
from jax import lax
from jax.experimental import pallas as pl
from jax.experimental.pallas import tpu as pltpu
from jax.sharding import PartitionSpec as P


FACET = 4096
SUB = 512
K = 128
FR = 512
NSUB = 4
W = 8
STEP = 64
GROUP = 8
MIDDLE = (SUB - W) // 2
HALF = SUB // 2
F32 = jnp.float32
BF16 = jnp.bfloat16
SMEM = pl.BlockSpec(memory_space=pltpu.SMEM)
VMEM = pl.BlockSpec(memory_space=pltpu.VMEM)
ANY = pl.BlockSpec(memory_space=pl.ANY)


def wave(turns, period):
    bits = period.bit_length() - 1
    phase = turns & (period - 1)
    quarter = (phase + period // 8) >> (bits - 2)
    theta = (phase - (quarter << (bits - 2))).astype(F32) * (2.0 * math.pi / period)
    square = theta * theta
    sine = theta * (
        1.0
        + square
        * (-1.0 / 6 + square * (1.0 / 120 + square * (-1.0 / 5040 + square * (1.0 / 362880))))
    )
    cosine = 1.0 + square * (
        -0.5
        + square
        * (1.0 / 24 + square * (-1.0 / 720 + square * (1.0 / 40320 - square * (1.0 / 3628800))))
    )
    odd = (quarter & 1) == 1
    real_part = jnp.where(odd, sine, cosine)
    imag_part = jnp.where(odd, cosine, sine)
    real_part = jnp.where(((quarter + 1) & 2) == 2, -real_part, real_part)
    imag_part = jnp.where((quarter & 2) == 2, -imag_part, imag_part)
    return real_part, imag_part


def turn(first, second, sky_cells, scale=1.0):
    real_part, imag_part = wave(first * second, sky_cells)
    return real_part * scale, imag_part * -scale


def amplitude(gap):
    top = wave(gap, 2 * SUB // K)[1]
    below = wave(gap, 2 * SUB)[1]
    return jnp.where(gap == 0, 1.0, top / (K * jnp.where(gap == 0, 1.0, below)))


def middle_of(start, sky_cells):
    return start + (K - 1) * (sky_cells // (2 * SUB))


def iota(shape, dimension):
    return lax.broadcasted_iota(jnp.int32, shape, dimension)


def expand(coarse_real, coarse_imag, fine_real, fine_imag):
    return (
        coarse_real * fine_real - coarse_imag * fine_imag,
        coarse_real * fine_imag + coarse_imag * fine_real,
    )


def parts_of(index):
    return slice(2 * index * K, (2 * index + 1) * K), slice((2 * index + 1) * K, (2 * index + 2) * K)


def tables_kernel(steps, geometry, meta, out_cols, out_rows, coarse_col, fine_col):
    sky_cells, row_spacing, copies = geometry
    count, columns = len(steps), out_cols.shape[1]
    facets = out_rows.shape[0] // count
    at_x, at_y = meta[0], meta[1]
    own = at_y // 2 // copies
    lane, row = iota((STEP, K), 1), iota((STEP, K), 0)
    re, im = parts_of(0)
    for s, step in enumerate(steps):
        chosen = own ^ step
        pair, (out_re, out_im) = s // 2, parts_of(s % 2)
        frequency = meta[2 + NSUB + chosen] + SUB // K * lane
        coarse_col[s, :, re], coarse_col[s, :, im] = turn(
            frequency, at_y * FACET + STEP * row, sky_cells, 1.0 / math.sqrt(FACET)
        )
        fine_col[:, re], fine_col[:, im] = turn(frequency, row, sky_cells)

        def table_turn(group, carry):
            coarse = coarse_col[s, pl.ds(pl.multiple_of(group * GROUP, GROUP), GROUP), :]
            for piece in range(GROUP):
                here = pl.ds(pl.multiple_of((group * GROUP + piece) * STEP, STEP), STEP)
                real_part, imag_part = expand(
                    coarse[piece : piece + 1, re],
                    coarse[piece : piece + 1, im],
                    fine_col[:, re],
                    fine_col[:, im],
                )
                out_cols[pair, here, out_re] = real_part.astype(BF16)
                out_cols[pair, here, out_im] = imag_part.astype(BF16)
            return carry

        lax.fori_loop(0, columns // (STEP * GROUP), table_turn, 0)
        frequency = meta[2 + chosen] + SUB // K * lane
        fine_real, fine_imag = turn(frequency, row, sky_cells)
        pieces = FR // STEP
        for a in range(facets):
            row_start = (at_x * facets + a) * row_spacing
            coarse_real, coarse_imag = turn(
                frequency[:pieces], row_start + STEP * row[:pieces], sky_cells, 1.0 / math.sqrt(FR)
            )
            for piece in range(pieces):
                here = slice(piece * STEP, (piece + 1) * STEP)
                real_part, imag_part = expand(
                    coarse_real[piece : piece + 1],
                    coarse_imag[piece : piece + 1],
                    fine_real,
                    fine_imag,
                )
                out_rows[s * facets + a, here, re] = real_part.astype(BF16)
                out_rows[s * facets + a, here, im] = imag_part.astype(BF16)


def strip_tables(meta, sky, steps, geometry):
    count, (rows, columns) = len(steps), sky.shape
    facets = rows // FR
    return pl.pallas_call(
        functools.partial(tables_kernel, steps, geometry),
        in_specs=[SMEM],
        out_specs=[VMEM] * 2,
        out_shape=[
            jax.ShapeDtypeStruct((count // 2, columns, 4 * K), BF16),
            jax.ShapeDtypeStruct((count * facets, FR, 2 * K), BF16),
        ],
        scratch_shapes=[
            pltpu.VMEM((count, columns // STEP, 2 * K), F32),
            pltpu.VMEM((STEP, 2 * K), F32),
        ],
        cost_estimate=pl.CostEstimate(flops=1 << 33, bytes_accessed=1 << 24, transcendentals=0),
        compiler_params=pltpu.CompilerParams(vmem_limit_bytes=16 << 20),
        name="strip_tables",
    )(meta)


def blocks_kernel(pair, sky, cols, rows, *outs):
    facets = sky.shape[0] // FR
    for a in range(facets):
        strips = jnp.dot(
            sky[a * FR : (a + 1) * FR, :], cols[pair], preferred_element_type=F32
        ).astype(BF16)
        for s in range(2):
            product = lax.dot_general(
                strips[:, 2 * s * K : (2 * s + 2) * K],
                rows[(2 * pair + s) * facets + a],
                (((0,), (0,)), ((), ())),
                preferred_element_type=F32,
            )
            re, im = parts_of(a)
            outs[s][:, re] = (product[:K, :K] - product[K:, K:]).astype(BF16)
            outs[s][:, im] = (product[:K, K:] + product[K:, :K]).astype(BF16)


def facet_blocks(sky, tables, pair):
    rows, columns = sky.shape
    facets = rows // FR
    return pl.pallas_call(
        functools.partial(blocks_kernel, pair),
        in_specs=[VMEM] * 3,
        out_specs=[VMEM] * 2,
        out_shape=[jax.ShapeDtypeStruct((K, 2 * facets * K), BF16)] * 2,
        cost_estimate=pl.CostEstimate(
            flops=8 * rows * columns * K, bytes_accessed=2 * rows * columns, transcendentals=0
        ),
        compiler_params=pltpu.CompilerParams(vmem_limit_bytes=28 << 20),
        name="facet_blocks",
    )(sky, *tables)


def col_table_kernel(geometry, factor, place, after, out):
    sky_cells, copies, sources = geometry
    planes = len(sources) * copies
    period = 2 * planes
    at_y = place[1]
    plane, core = at_y // 2, at_y % 2
    own = plane // copies
    gap = core * HALF + iota((HALF, K), 0) - SUB // K * iota((HALF, K), 1)
    size = amplitude(gap) * factor
    real_part, imag_part = wave(gap * middle_of(0, sky_cells), sky_cells)
    folded = (HALF // period, period, K)
    real_part = (size * real_part).reshape(folded)
    imag_part = (size * imag_part).reshape(folded)
    steps = gap[:period]
    at = 0
    for other in range(2):
        for step in sources:
            for copy_step in range(copies):
                source = (own ^ step) * copies + (plane % copies ^ copy_step)
                turned = wave(steps * (2 * source + (core + other) % 2), period)
                both = expand(real_part, imag_part, turned[0][None], turned[1][None])
                out[at, :HALF, :] = both[0].reshape(HALF, K).astype(BF16)
                out[at, HALF:, :] = both[1].reshape(HALF, K).astype(BF16)
                at += 1


def row_table_kernel(geometry, place, after, out):
    sky_cells, facets, rows_axis = geometry
    period = facets * rows_axis
    gap = iota((K, SUB), 1) - SUB // K * iota((K, SUB), 0)
    size = amplitude(gap)
    real_part, imag_part = wave(gap * middle_of(0, sky_cells), sky_cells)
    folded = (K // period, period, SUB)
    real_part = (size * real_part).reshape(folded)
    imag_part = (size * imag_part).reshape(folded)
    steps = gap[:period]
    for source in range(period):
        step, a = source // facets, source % facets
        facet_row = (place[0] ^ step) * facets + a
        turned = wave(steps * facet_row, period)
        both = expand(real_part, imag_part, turned[0][None], turned[1][None])
        out[source, :, :SUB] = both[0].reshape(K, SUB).astype(BF16)
        out[source, :, SUB:] = both[1].reshape(K, SUB).astype(BF16)


def columns_kernel(count, facets, table, *refs):
    blocks, out = refs[:count], refs[count]
    total = None
    for pair in range(0, count, 2):
        stacked = jnp.concatenate([block[...] for block in blocks[pair : pair + 2]], axis=0)
        turned = jnp.concatenate([table[at] for at in range(pair, min(pair + 2, count))], axis=1)
        part = jnp.dot(turned, stacked, preferred_element_type=F32)
        total = part if total is None else total + part
    for a in range(facets):
        re, im = parts_of(a)
        out[:HALF, a * K : (a + 1) * K] = (total[:HALF, re] - total[HALF:, im]).astype(BF16)
        out[HALF:, a * K : (a + 1) * K] = (total[:HALF, im] + total[HALF:, re]).astype(BF16)


def column_sums(table, blocks):
    facets = blocks[0].shape[1] // (2 * K)
    return pl.pallas_call(
        functools.partial(columns_kernel, len(blocks), facets),
        out_shape=jax.ShapeDtypeStruct((2 * HALF, facets * K), BF16),
        cost_estimate=pl.CostEstimate(
            flops=8 * HALF * len(blocks) * facets * K * K, bytes_accessed=1 << 21, transcendentals=0
        ),
        compiler_params=pltpu.CompilerParams(vmem_limit_bytes=20 << 20),
        name="column_sums",
    )(table, *blocks)


def taps_of(first, kernel, shape):
    row = iota(shape, 0)
    tap = (row - first) & (W - 1)
    value = jnp.zeros(shape, F32)
    for e in range(W):
        value = jnp.where(tap == e, kernel[e : e + 1, :], value)
    return value, (first - row + (W - 1)) >> 3


def query_kernel(vis_cells, row_kernel, col_kernel, after, out):
    count = vis_cells.shape[1]
    out[:, :count] = row_kernel[...]
    out[:, count : 2 * count] = col_kernel[...].astype(BF16)
    cells = (vis_cells[...] - MIDDLE).astype(F32)
    quarters = [
        cells[axis : axis + 1, at * count // 4 : (at + 1) * count // 4]
        for axis in range(2)
        for at in range(4)
    ]
    out[:, 2 * count :] = jnp.concatenate(quarters, axis=0).astype(BF16)


def row_sums(sums, table):
    total = None
    facets = sums[0].shape[1] // K
    for source, part in enumerate(sums):
        turned = jnp.concatenate(
            [table[at] for at in range(source * facets, (source + 1) * facets)], axis=0
        )
        part = jnp.dot(part[...], turned, preferred_element_type=F32)
        total = part if total is None else total + part
    return total


def partial_kernel(table, *refs):
    refs[-1][...] = row_sums(refs[:-1], table)


def degrid_kernel(geometry, place, readers, table, partial, last, queries_own, queries_other, *refs):
    cols_axis, copies = geometry
    outs, subgrid = refs[:2], refs[2]
    at_x, at_y = place[0], place[1]
    plane, core = at_y // 2, at_y % 2
    own = plane // copies
    facets = last.shape[1] // K
    total = partial[...] + row_sums([last], table[table.shape[0] - facets :])
    subgrid[:HALF, :] = (total[:HALF, :SUB] - total[HALF:, SUB:]).astype(BF16)
    subgrid[HALF:, :] = (total[:HALF, SUB:] + total[HALF:, :SUB]).astype(BF16)
    planes = queries_own.shape[0]
    count = outs[0].shape[2]
    for other, (queries, out) in enumerate(zip((queries_own, queries_other), outs)):

        def slot_turn(slot, carry):
            source = plane ^ slot
            reader = at_x * cols_axis + 2 * source + (core + other) % 2
            active = (readers[reader] == own) & (source % copies == plane % copies)

            @pl.when(jnp.logical_not(active))
            def _():
                out[slot] = jnp.zeros(out.shape[1:], F32)

            @pl.when(active)
            def _():
                values = queries[slot].astype(F32)
                cells = values[:, 2 * count :].astype(jnp.int32) + MIDDLE
                u, w = [
                    jnp.concatenate([cells[4 * axis + at : 4 * axis + at + 1] for at in range(4)], axis=1)
                    for axis in range(2)
                ]
                row_value, row_group = taps_of(u, values[:, :count], (W, count))
                groups = iota((SUB // W, W, count), 0)
                weights = jnp.where(groups == row_group[None], row_value[None], 0.0)
                weights = weights.reshape(SUB, count).astype(BF16)
                spread = jnp.dot(subgrid[...], weights, preferred_element_type=F32)
                spread = spread.reshape(2, HALF // W, W, count)
                col_value, col_group = taps_of(w, values[:, count : 2 * count], (W, count))
                groups = iota((HALF // W, W, count), 0)
                hit = groups == (col_group - core * (HALF // W))[None]
                for p in range(2):
                    picked = jnp.sum(jnp.where(hit, spread[p], 0.0), axis=0)
                    out[slot, p : p + 1, :] = jnp.sum(picked * col_value, axis=0, keepdims=True)

            return carry

        lax.fori_loop(0, planes, slot_turn, 0)


def degrid(place, readers, table, partial, last, queries, others, geometry):
    planes, _, width = queries.shape
    result = jax.ShapeDtypeStruct((planes, 2, width * 4 // 9), F32)
    return pl.pallas_call(
        functools.partial(degrid_kernel, geometry),
        in_specs=[SMEM, SMEM] + [VMEM] * 5,
        out_specs=[VMEM, VMEM],
        out_shape=[result, result],
        scratch_shapes=[pltpu.VMEM((2 * HALF, SUB), BF16)],
        cost_estimate=pl.CostEstimate(flops=1 << 33, bytes_accessed=1 << 22, transcendentals=0),
        compiler_params=pltpu.CompilerParams(vmem_limit_bytes=24 << 20),
        name="degrid",
    )(place, readers, table, partial, last, queries, others)


def local(sky, sub_off, readers, vis_cells, row_kernel, col_kernel):
    rows_axis = lax.axis_size("fx")
    cols_axis = lax.axis_size("fy")
    planes = cols_axis // 2
    copies = planes // NSUB
    facets = sky.shape[0] // FR
    sky_cells = FACET * cols_axis
    facet_rows = facets * rows_axis
    row_spacing = sky_cells // facet_rows
    factor = 1.0 / math.sqrt(facet_rows * cols_axis)
    assert planes == copies * NSUB and not any(
        size & (size - 1) for size in (sky_cells, rows_axis, copies)
    )
    place = jnp.stack([lax.axis_index("fx"), lax.axis_index("fy")]).astype(jnp.int32)
    meta = jnp.concatenate([place, sub_off.reshape(-1)])

    def plane_shift(group_step, copy_step):
        moved = []
        for z in range(planes):
            to = (z // copies ^ group_step) * copies + (z % copies ^ copy_step)
            moved += [(2 * z + c, 2 * to + c) for c in range(2)]
        return moved

    swap = [(i, i ^ 1) for i in range(cols_axis)]

    steps = [*range(2, NSUB), 1, 0]
    tables = strip_tables(meta, sky, steps, (sky_cells, row_spacing, copies))
    blocks = []
    for start in range(0, NSUB, 2):
        pair = facet_blocks(sky, tables, start // 2)
        for step, block in zip(steps[start : start + 2], pair):
            for copy_step in range(copies):
                moved = block
                if step or copy_step:
                    moved = lax.ppermute(block, "fy", plane_shift(step, copy_step))
                blocks.append(moved)
    col_table = pl.pallas_call(
        functools.partial(col_table_kernel, (sky_cells, copies, steps), factor),
        in_specs=[SMEM, ANY],
        out_specs=VMEM,
        out_shape=jax.ShapeDtypeStruct((2 * len(blocks), 2 * HALF, K), BF16),
        cost_estimate=pl.CostEstimate(flops=1 << 22, bytes_accessed=1 << 20, transcendentals=1 << 20),
        compiler_params=pltpu.CompilerParams(vmem_limit_bytes=20 << 20),
        name="col_table",
    )(place, pair[0])
    query = pl.pallas_call(
        query_kernel,
        in_specs=[VMEM, VMEM, VMEM, ANY],
        out_specs=VMEM,
        out_shape=jax.ShapeDtypeStruct((W, vis_cells.shape[1] * 9 // 4), BF16),
        compiler_params=pltpu.CompilerParams(vmem_limit_bytes=20 << 20),
        name="query",
    )(vis_cells, row_kernel, col_kernel, pair[0])
    *blocks[: 2 * copies], _ = lax.optimization_barrier((*blocks[: 2 * copies], col_table))
    blocks += [lax.ppermute(block, "fy", swap) for block in blocks]
    sums = [column_sums(col_table, blocks)]

    for step in range(1, rows_axis):
        sums.append(lax.ppermute(sums[0], "fx", [(i, i ^ step) for i in range(rows_axis)]))
    row_table = pl.pallas_call(
        functools.partial(row_table_kernel, (sky_cells, facets, rows_axis)),
        in_specs=[SMEM, ANY],
        out_specs=VMEM,
        out_shape=jax.ShapeDtypeStruct((facet_rows, K, 2 * SUB), BF16),
        cost_estimate=pl.CostEstimate(
            flops=1 << 23, bytes_accessed=1 << 21, transcendentals=1 << 21
        ),
        compiler_params=pltpu.CompilerParams(vmem_limit_bytes=20 << 20),
        name="row_table",
    )(place, sums[0])

    moved, _ = lax.optimization_barrier((query, sums[0]))
    queries = [query]
    for step in range(1, planes):
        ring = [(i, i ^ 2 * step) for i in range(cols_axis)]
        queries.append(lax.ppermute(moved, "fy", ring))
    queries = jnp.stack(queries)
    others = lax.ppermute(queries, "fy", swap)
    partial = pl.pallas_call(
        partial_kernel,
        in_specs=[VMEM] * rows_axis,
        out_specs=VMEM,
        out_shape=jax.ShapeDtypeStruct((2 * HALF, 2 * SUB), F32),
        cost_estimate=pl.CostEstimate(
            flops=8 * HALF * SUB * facet_rows * K, bytes_accessed=1 << 22, transcendentals=0
        ),
        compiler_params=pltpu.CompilerParams(vmem_limit_bytes=20 << 20),
        name="partial_rows",
    )(row_table, *sums[:-1])
    results, others = degrid(
        place, readers, row_table, partial, sums[-1], queries, others, (cols_axis, copies)
    )

    both = results + lax.ppermute(others, "fy", swap)
    vis = both[0]
    for step in range(1, planes):
        ring = [(i, i ^ 2 * step) for i in range(cols_axis)]
        vis = vis + lax.ppermute(both[step], "fy", ring)
    return vis


def solution(mesh):
    return jax.shard_map(
        local,
        mesh=mesh,
        in_specs=(
            P("fx", "fy"),
            P(),
            P(),
            P(None, ("fx", "fy")),
            P(None, ("fx", "fy")),
            P(None, ("fx", "fy")),
        ),
        out_specs=P(None, ("fx", "fy")),
        check_vma=False,
    )
```

```python
import functools
import math

import jax
import jax.numpy as jnp
from jax import lax
from jax.experimental import pallas as pl
from jax.experimental.pallas import tpu as pltpu
from jax.sharding import PartitionSpec as P


FACET = 4096
SUB = 512
K = 128
FR = 512
NSUB = 4
W = 8
STEP = 64
GROUP = 8
TILE = 16
MIDDLE = (SUB - W) // 2
HALF = SUB // 2
F32 = jnp.float32
BF16 = jnp.bfloat16
SMEM = pl.BlockSpec(memory_space=pltpu.SMEM)
VMEM = pl.BlockSpec(memory_space=pltpu.VMEM)
ANY = pl.BlockSpec(memory_space=pl.ANY)


def wave(turns, period):
    bits = period.bit_length() - 1
    phase = turns & (period - 1)
    quarter = (phase + period // 8) >> (bits - 2)
    theta = (phase - (quarter << (bits - 2))).astype(F32) * (2.0 * math.pi / period)
    square = theta * theta
    sine = theta * (
        1.0
        + square
        * (-1.0 / 6 + square * (1.0 / 120 + square * (-1.0 / 5040 + square * (1.0 / 362880))))
    )
    cosine = 1.0 + square * (
        -0.5
        + square
        * (1.0 / 24 + square * (-1.0 / 720 + square * (1.0 / 40320 - square * (1.0 / 3628800))))
    )
    odd = (quarter & 1) == 1
    real_part = jnp.where(odd, sine, cosine)
    imag_part = jnp.where(odd, cosine, sine)
    real_part = jnp.where(((quarter + 1) & 2) == 2, -real_part, real_part)
    imag_part = jnp.where((quarter & 2) == 2, -imag_part, imag_part)
    return real_part, imag_part


def turn(first, second, sky_cells, scale=1.0):
    real_part, imag_part = wave(first * second, sky_cells)
    return real_part * scale, imag_part * -scale


def amplitude(gap):
    top = wave(gap, 2 * SUB // K)[1]
    below = wave(gap, 2 * SUB)[1]
    return jnp.where(gap == 0, 1.0, top / (K * jnp.where(gap == 0, 1.0, below)))


def middle_of(start, sky_cells):
    return start + (K - 1) * (sky_cells // (2 * SUB))


def iota(shape, dimension):
    return lax.broadcasted_iota(jnp.int32, shape, dimension)


def expand(coarse_real, coarse_imag, fine_real, fine_imag):
    return (
        coarse_real * fine_real - coarse_imag * fine_imag,
        coarse_real * fine_imag + coarse_imag * fine_real,
    )


def parts_of(index):
    return slice(2 * index * K, (2 * index + 1) * K), slice((2 * index + 1) * K, (2 * index + 2) * K)


def tables_kernel(steps, geometry, meta, out_cols, out_rows, coarse_col, fine_col):
    sky_cells, row_spacing, copies = geometry
    count, columns = len(steps), out_cols.shape[0]
    facets = out_rows.shape[0] // count
    at_x, at_y = meta[0], meta[1]
    own = at_y // 2 // copies
    lane, row = iota((STEP, K), 1), iota((STEP, K), 0)
    re, im = parts_of(0)
    for s, step in enumerate(steps):
        chosen = own ^ step
        out_re, out_im = parts_of(s)
        frequency = meta[2 + NSUB + chosen] + SUB // K * lane
        coarse_col[s, :, re], coarse_col[s, :, im] = turn(
            frequency, at_y * FACET + STEP * row, sky_cells, 1.0 / math.sqrt(FACET)
        )
        fine_col[:, re], fine_col[:, im] = turn(frequency, row, sky_cells)

        def table_turn(group, carry):
            coarse = coarse_col[s, pl.ds(pl.multiple_of(group * GROUP, GROUP), GROUP), :]
            for tile in range(0, STEP, TILE):
                fine_real, fine_imag = fine_col[tile : tile + TILE, re], fine_col[tile : tile + TILE, im]
                for piece in range(GROUP):
                    here = pl.ds(pl.multiple_of((group * GROUP + piece) * STEP + tile, TILE), TILE)
                    real_part, imag_part = expand(
                        coarse[piece : piece + 1, re],
                        coarse[piece : piece + 1, im],
                        fine_real,
                        fine_imag,
                    )
                    out_cols[here, out_re] = real_part.astype(BF16)
                    out_cols[here, out_im] = imag_part.astype(BF16)
            return carry

        lax.fori_loop(0, columns // (STEP * GROUP), table_turn, 0)
        frequency = meta[2 + chosen] + SUB // K * lane
        fine_real, fine_imag = turn(frequency, row, sky_cells)
        pieces = FR // STEP
        for a in range(facets):
            row_start = (at_x * facets + a) * row_spacing
            coarse_real, coarse_imag = turn(
                frequency[:pieces], row_start + STEP * row[:pieces], sky_cells, 1.0 / math.sqrt(FR)
            )
            for piece in range(pieces):
                here = slice(piece * STEP, (piece + 1) * STEP)
                real_part, imag_part = expand(
                    coarse_real[piece : piece + 1],
                    coarse_imag[piece : piece + 1],
                    fine_real,
                    fine_imag,
                )
                out_rows[s * facets + a, here, re] = real_part.astype(BF16)
                out_rows[s * facets + a, here, im] = imag_part.astype(BF16)


def strip_tables(meta, sky, steps, geometry):
    count, (rows, columns) = len(steps), sky.shape
    facets = rows // FR
    return pl.pallas_call(
        functools.partial(tables_kernel, steps, geometry),
        in_specs=[SMEM],
        out_specs=[VMEM] * 2,
        out_shape=[
            jax.ShapeDtypeStruct((columns, 2 * count * K), BF16),
            jax.ShapeDtypeStruct((count * facets, FR, 2 * K), BF16),
        ],
        scratch_shapes=[
            pltpu.VMEM((count, columns // STEP, 2 * K), F32),
            pltpu.VMEM((STEP, 2 * K), F32),
        ],
        cost_estimate=pl.CostEstimate(flops=1 << 33, bytes_accessed=1 << 24, transcendentals=0),
        compiler_params=pltpu.CompilerParams(vmem_limit_bytes=16 << 20),
        name="strip_tables",
    )(meta)


def blocks_kernel(at, sky, cols, rows, out):
    facets = sky.shape[0] // FR
    strips = jnp.dot(
        sky[...], cols[:, 2 * at * K : 2 * (at + 1) * K], preferred_element_type=F32
    ).astype(BF16)
    for a in range(facets):
        product = lax.dot_general(
            strips[a * FR : (a + 1) * FR, :],
            rows[at * facets + a],
            (((0,), (0,)), ((), ())),
            preferred_element_type=F32,
        )
        re, im = parts_of(a)
        out[:, re] = (product[:K, :K] - product[K:, K:]).astype(BF16)
        out[:, im] = (product[:K, K:] + product[K:, :K]).astype(BF16)


def facet_blocks(sky, tables, at):
    rows, columns = sky.shape
    return pl.pallas_call(
        functools.partial(blocks_kernel, at),
        in_specs=[VMEM] * 3,
        out_specs=VMEM,
        out_shape=jax.ShapeDtypeStruct((K, 2 * rows // FR * K), BF16),
        cost_estimate=pl.CostEstimate(
            flops=4 * rows * columns * K, bytes_accessed=2 * rows * columns, transcendentals=0
        ),
        compiler_params=pltpu.CompilerParams(vmem_limit_bytes=28 << 20),
        name="facet_blocks",
    )(sky, *tables)


def col_table_kernel(geometry, factor, place, after, out):
    sky_cells, copies, sources = geometry
    planes = len(sources) * copies
    period = 2 * planes
    at_y = place[1]
    plane, core = at_y // 2, at_y % 2
    own = plane // copies
    gap = core * HALF + iota((HALF, K), 0) - SUB // K * iota((HALF, K), 1)
    size = amplitude(gap) * factor
    real_part, imag_part = wave(gap * middle_of(0, sky_cells), sky_cells)
    folded = (HALF // period, period, K)
    real_part = (size * real_part).reshape(folded)
    imag_part = (size * imag_part).reshape(folded)
    steps = gap[:period]
    at = 0
    for other in range(2):
        for step in sources:
            for copy_step in range(copies):
                source = (own ^ step) * copies + (plane % copies ^ copy_step)
                turned = wave(steps * (2 * source + (core + other) % 2), period)
                both = expand(real_part, imag_part, turned[0][None], turned[1][None])
                out[at, :HALF, :] = both[0].reshape(HALF, K).astype(BF16)
                out[at, HALF:, :] = both[1].reshape(HALF, K).astype(BF16)
                at += 1


def row_table_kernel(geometry, place, after, out):
    sky_cells, facets, rows_axis = geometry
    period = facets * rows_axis
    gap = iota((K, SUB), 1) - SUB // K * iota((K, SUB), 0)
    size = amplitude(gap)
    real_part, imag_part = wave(gap * middle_of(0, sky_cells), sky_cells)
    folded = (K // period, period, SUB)
    real_part = (size * real_part).reshape(folded)
    imag_part = (size * imag_part).reshape(folded)
    steps = gap[:period]
    for source in range(period):
        step, a = source // facets, source % facets
        facet_row = (place[0] ^ step) * facets + a
        turned = wave(steps * facet_row, period)
        both = expand(real_part, imag_part, turned[0][None], turned[1][None])
        out[source, :, :SUB] = both[0].reshape(K, SUB).astype(BF16)
        out[source, :, SUB:] = both[1].reshape(K, SUB).astype(BF16)


def columns_kernel(count, facets, table, *refs):
    blocks, out = refs[:count], refs[count]
    total = None
    for pair in range(0, count, 2):
        stacked = jnp.concatenate([block[...] for block in blocks[pair : pair + 2]], axis=0)
        turned = jnp.concatenate([table[at] for at in range(pair, min(pair + 2, count))], axis=1)
        part = jnp.dot(turned, stacked, preferred_element_type=F32)
        total = part if total is None else total + part
    for a in range(facets):
        re, im = parts_of(a)
        out[:HALF, a * K : (a + 1) * K] = (total[:HALF, re] - total[HALF:, im]).astype(BF16)
        out[HALF:, a * K : (a + 1) * K] = (total[:HALF, im] + total[HALF:, re]).astype(BF16)


def column_sums(table, blocks):
    facets = blocks[0].shape[1] // (2 * K)
    return pl.pallas_call(
        functools.partial(columns_kernel, len(blocks), facets),
        out_shape=jax.ShapeDtypeStruct((2 * HALF, facets * K), BF16),
        cost_estimate=pl.CostEstimate(
            flops=8 * HALF * len(blocks) * facets * K * K, bytes_accessed=1 << 21, transcendentals=0
        ),
        compiler_params=pltpu.CompilerParams(vmem_limit_bytes=20 << 20),
        name="column_sums",
    )(table, *blocks)


def taps_of(first, kernel, shape):
    row = iota(shape, 0)
    tap = (row - first) & (W - 1)
    value = jnp.zeros(shape, F32)
    for e in range(W):
        value = jnp.where(tap == e, kernel[e : e + 1, :], value)
    return value, (first - row + (W - 1)) >> 3


def query_kernel(vis_cells, row_kernel, col_kernel, after, out):
    count = vis_cells.shape[1]
    out[:, :count] = row_kernel[...]
    out[:, count : 2 * count] = col_kernel[...].astype(BF16)
    cells = (vis_cells[...] - MIDDLE).astype(F32)
    quarters = [
        cells[axis : axis + 1, at * count // 4 : (at + 1) * count // 4]
        for axis in range(2)
        for at in range(4)
    ]
    out[:, 2 * count :] = jnp.concatenate(quarters, axis=0).astype(BF16)


def row_sums(sums, table):
    total = None
    facets = sums[0].shape[1] // K
    for source, part in enumerate(sums):
        turned = jnp.concatenate(
            [table[at] for at in range(source * facets, (source + 1) * facets)], axis=0
        )
        part = jnp.dot(part[...], turned, preferred_element_type=F32)
        total = part if total is None else total + part
    return total


def partial_kernel(table, *refs):
    refs[-1][...] = row_sums(refs[:-1], table)


def degrid_kernel(geometry, place, readers, table, partial, last, queries_own, queries_other, *refs):
    cols_axis, copies = geometry
    outs, subgrid = refs[:2], refs[2]
    at_x, at_y = place[0], place[1]
    plane, core = at_y // 2, at_y % 2
    own = plane // copies
    facets = last.shape[1] // K
    total = partial[...] + row_sums([last], table[table.shape[0] - facets :])
    subgrid[:HALF, :] = (total[:HALF, :SUB] - total[HALF:, SUB:]).astype(BF16)
    subgrid[HALF:, :] = (total[:HALF, SUB:] + total[HALF:, :SUB]).astype(BF16)
    planes = queries_own.shape[0]
    count = outs[0].shape[2]
    for other, (queries, out) in enumerate(zip((queries_own, queries_other), outs)):

        def slot_turn(slot, carry):
            source = plane ^ slot
            reader = at_x * cols_axis + 2 * source + (core + other) % 2
            active = (readers[reader] == own) & (source % copies == plane % copies)

            @pl.when(jnp.logical_not(active))
            def _():
                out[slot] = jnp.zeros(out.shape[1:], F32)

            @pl.when(active)
            def _():
                values = queries[slot].astype(F32)
                cells = values[:, 2 * count :].astype(jnp.int32) + MIDDLE
                u, w = [
                    jnp.concatenate([cells[4 * axis + at : 4 * axis + at + 1] for at in range(4)], axis=1)
                    for axis in range(2)
                ]
                row_value, row_group = taps_of(u, values[:, :count], (W, count))
                groups = iota((SUB // W, W, count), 0)
                weights = jnp.where(groups == row_group[None], row_value[None], 0.0)
                weights = weights.reshape(SUB, count).astype(BF16)
                spread = jnp.dot(subgrid[...], weights, preferred_element_type=F32)
                spread = spread.reshape(2, HALF // W, W, count)
                col_value, col_group = taps_of(w, values[:, count : 2 * count], (W, count))
                groups = iota((HALF // W, W, count), 0)
                hit = groups == (col_group - core * (HALF // W))[None]
                for p in range(2):
                    picked = jnp.sum(jnp.where(hit, spread[p], 0.0), axis=0)
                    out[slot, p : p + 1, :] = jnp.sum(picked * col_value, axis=0, keepdims=True)

            return carry

        lax.fori_loop(0, planes, slot_turn, 0)


def degrid(place, readers, table, partial, last, queries, others, geometry):
    planes, _, width = queries.shape
    result = jax.ShapeDtypeStruct((planes, 2, width * 4 // 9), F32)
    return pl.pallas_call(
        functools.partial(degrid_kernel, geometry),
        in_specs=[SMEM, SMEM] + [VMEM] * 5,
        out_specs=[VMEM, VMEM],
        out_shape=[result, result],
        scratch_shapes=[pltpu.VMEM((2 * HALF, SUB), BF16)],
        cost_estimate=pl.CostEstimate(flops=1 << 33, bytes_accessed=1 << 22, transcendentals=0),
        compiler_params=pltpu.CompilerParams(vmem_limit_bytes=24 << 20),
        name="degrid",
    )(place, readers, table, partial, last, queries, others)


def local(sky, sub_off, readers, vis_cells, row_kernel, col_kernel):
    rows_axis = lax.axis_size("fx")
    cols_axis = lax.axis_size("fy")
    planes = cols_axis // 2
    copies = planes // NSUB
    facets = sky.shape[0] // FR
    sky_cells = FACET * cols_axis
    facet_rows = facets * rows_axis
    row_spacing = sky_cells // facet_rows
    factor = 1.0 / math.sqrt(facet_rows * cols_axis)
    assert planes == copies * NSUB and not any(
        size & (size - 1) for size in (sky_cells, rows_axis, copies)
    )
    place = jnp.stack([lax.axis_index("fx"), lax.axis_index("fy")]).astype(jnp.int32)
    meta = jnp.concatenate([place, sub_off.reshape(-1)])

    def plane_shift(group_step, copy_step):
        moved = []
        for z in range(planes):
            to = (z // copies ^ group_step) * copies + (z % copies ^ copy_step)
            moved += [(2 * z + c, 2 * to + c) for c in range(2)]
        return moved

    swap = [(i, i ^ 1) for i in range(cols_axis)]

    steps = [*range(2, NSUB), 1, 0]
    blocks = []
    for start in range(0, NSUB, 2):
        tables = strip_tables(meta, sky, steps[start : start + 2], (sky_cells, row_spacing, copies))
        for at, step in enumerate(steps[start : start + 2]):
            block = facet_blocks(sky, tables, at)
            for copy_step in range(copies):
                moved = block
                if step or copy_step:
                    moved = lax.ppermute(block, "fy", plane_shift(step, copy_step))
                blocks.append(moved)

    col_table = pl.pallas_call(
        functools.partial(col_table_kernel, (sky_cells, copies, steps), factor),
        in_specs=[SMEM, ANY],
        out_specs=VMEM,
        out_shape=jax.ShapeDtypeStruct((2 * len(blocks), 2 * HALF, K), BF16),
        cost_estimate=pl.CostEstimate(flops=1 << 22, bytes_accessed=1 << 20, transcendentals=1 << 20),
        compiler_params=pltpu.CompilerParams(vmem_limit_bytes=20 << 20),
        name="col_table",
    )(place, block)
    query = pl.pallas_call(
        query_kernel,
        in_specs=[VMEM, VMEM, VMEM, ANY],
        out_specs=VMEM,
        out_shape=jax.ShapeDtypeStruct((W, vis_cells.shape[1] * 9 // 4), BF16),
        compiler_params=pltpu.CompilerParams(vmem_limit_bytes=20 << 20),
        name="query",
    )(vis_cells, row_kernel, col_kernel, block)
    *blocks[: 2 * copies], _ = lax.optimization_barrier((*blocks[: 2 * copies], col_table))
    blocks += [lax.ppermute(block, "fy", swap) for block in blocks]
    sums = [column_sums(col_table, blocks)]

    for step in range(1, rows_axis):
        sums.append(lax.ppermute(sums[0], "fx", [(i, i ^ step) for i in range(rows_axis)]))
    row_table = pl.pallas_call(
        functools.partial(row_table_kernel, (sky_cells, facets, rows_axis)),
        in_specs=[SMEM, ANY],
        out_specs=VMEM,
        out_shape=jax.ShapeDtypeStruct((facet_rows, K, 2 * SUB), BF16),
        cost_estimate=pl.CostEstimate(
            flops=1 << 23, bytes_accessed=1 << 21, transcendentals=1 << 21
        ),
        compiler_params=pltpu.CompilerParams(vmem_limit_bytes=20 << 20),
        name="row_table",
    )(place, sums[0])

    moved, _ = lax.optimization_barrier((query, sums[0]))
    queries = [query]
    for step in range(1, planes):
        ring = [(i, i ^ 2 * step) for i in range(cols_axis)]
        queries.append(lax.ppermute(moved, "fy", ring))
    queries = jnp.stack(queries)
    others = lax.ppermute(queries, "fy", swap)
    partial = pl.pallas_call(
        partial_kernel,
        in_specs=[VMEM] * rows_axis,
        out_specs=VMEM,
        out_shape=jax.ShapeDtypeStruct((2 * HALF, 2 * SUB), F32),
        cost_estimate=pl.CostEstimate(
            flops=8 * HALF * SUB * facet_rows * K, bytes_accessed=1 << 22, transcendentals=0
        ),
        compiler_params=pltpu.CompilerParams(vmem_limit_bytes=20 << 20),
        name="partial_rows",
    )(row_table, *sums[:-1])
    results, others = degrid(
        place, readers, row_table, partial, sums[-1], queries, others, (cols_axis, copies)
    )

    both = results + lax.ppermute(others, "fy", swap)
    vis = both[0]
    for step in range(1, planes):
        ring = [(i, i ^ 2 * step) for i in range(cols_axis)]
        vis = vis + lax.ppermute(both[step], "fy", ring)
    return vis


def solution(mesh):
    return jax.shard_map(
        local,
        mesh=mesh,
        in_specs=(
            P("fx", "fy"),
            P(),
            P(),
            P(None, ("fx", "fy")),
            P(None, ("fx", "fy")),
            P(None, ("fx", "fy")),
        ),
        out_specs=P(None, ("fx", "fy")),
        check_vma=False,
    )
```

```python
import functools
import math

import jax
import jax.numpy as jnp
from jax import lax
from jax.experimental import pallas as pl
from jax.experimental.pallas import tpu as pltpu
from jax.sharding import PartitionSpec as P


FACET = 4096
SUB = 512
K = 128
FR = 512
NSUB = 4
W = 8
STEP = 64
GROUP = 8
TILE = 16
MIDDLE = (SUB - W) // 2
HALF = SUB // 2
F32 = jnp.float32
BF16 = jnp.bfloat16
SMEM = pl.BlockSpec(memory_space=pltpu.SMEM)
VMEM = pl.BlockSpec(memory_space=pltpu.VMEM)
ANY = pl.BlockSpec(memory_space=pl.ANY)


def wave(turns, period):
    bits = period.bit_length() - 1
    phase = turns & (period - 1)
    quarter = (phase + period // 8) >> (bits - 2)
    theta = (phase - (quarter << (bits - 2))).astype(F32) * (2.0 * math.pi / period)
    square = theta * theta
    sine = theta * (
        1.0
        + square
        * (-1.0 / 6 + square * (1.0 / 120 + square * (-1.0 / 5040 + square * (1.0 / 362880))))
    )
    cosine = 1.0 + square * (
        -0.5
        + square
        * (1.0 / 24 + square * (-1.0 / 720 + square * (1.0 / 40320 - square * (1.0 / 3628800))))
    )
    odd = (quarter & 1) == 1
    real_part = jnp.where(odd, sine, cosine)
    imag_part = jnp.where(odd, cosine, sine)
    real_part = jnp.where(((quarter + 1) & 2) == 2, -real_part, real_part)
    imag_part = jnp.where((quarter & 2) == 2, -imag_part, imag_part)
    return real_part, imag_part


def turn(first, second, sky_cells, scale=1.0):
    real_part, imag_part = wave(first * second, sky_cells)
    return real_part * scale, imag_part * -scale


def amplitude(gap):
    top = wave(gap, 2 * SUB // K)[1]
    below = wave(gap, 2 * SUB)[1]
    return jnp.where(gap == 0, 1.0, top / (K * jnp.where(gap == 0, 1.0, below)))


def middle_of(start, sky_cells):
    return start + (K - 1) * (sky_cells // (2 * SUB))


def iota(shape, dimension):
    return lax.broadcasted_iota(jnp.int32, shape, dimension)


def expand(coarse_real, coarse_imag, fine_real, fine_imag):
    return (
        coarse_real * fine_real - coarse_imag * fine_imag,
        coarse_real * fine_imag + coarse_imag * fine_real,
    )


def parts_of(index):
    return slice(2 * index * K, (2 * index + 1) * K), slice((2 * index + 1) * K, (2 * index + 2) * K)


def tables_kernel(steps, geometry, meta, out_cols, out_rows, coarse_col, fine_col):
    sky_cells, row_spacing, copies = geometry
    count, columns = len(steps), out_cols.shape[0]
    facets = out_rows.shape[0] // count
    at_x, at_y = meta[0], meta[1]
    own = at_y // 2 // copies
    lane, row = iota((STEP, K), 1), iota((STEP, K), 0)
    re, im = parts_of(0)
    for s, step in enumerate(steps):
        chosen = own ^ step
        out_re, out_im = parts_of(s)
        frequency = meta[2 + NSUB + chosen] + SUB // K * lane
        coarse_col[s, :, re], coarse_col[s, :, im] = turn(
            frequency, at_y * FACET + STEP * row, sky_cells, 1.0 / math.sqrt(FACET)
        )
        fine_col[:, re], fine_col[:, im] = turn(frequency, row, sky_cells)

        def table_turn(group, carry):
            coarse = coarse_col[s, pl.ds(pl.multiple_of(group * GROUP, GROUP), GROUP), :]
            for tile in range(0, STEP, TILE):
                fine_real, fine_imag = fine_col[tile : tile + TILE, re], fine_col[tile : tile + TILE, im]
                for piece in range(GROUP):
                    here = pl.ds(pl.multiple_of((group * GROUP + piece) * STEP + tile, TILE), TILE)
                    real_part, imag_part = expand(
                        coarse[piece : piece + 1, re],
                        coarse[piece : piece + 1, im],
                        fine_real,
                        fine_imag,
                    )
                    out_cols[here, out_re] = real_part.astype(BF16)
                    out_cols[here, out_im] = imag_part.astype(BF16)
            return carry

        lax.fori_loop(0, columns // (STEP * GROUP), table_turn, 0)
        frequency = meta[2 + chosen] + SUB // K * lane
        fine_real, fine_imag = turn(frequency, row, sky_cells)
        pieces = FR // STEP
        for a in range(facets):
            row_start = (at_x * facets + a) * row_spacing
            coarse_real, coarse_imag = turn(
                frequency[:pieces], row_start + STEP * row[:pieces], sky_cells, 1.0 / math.sqrt(FR)
            )
            for piece in range(pieces):
                here = slice(piece * STEP, (piece + 1) * STEP)
                real_part, imag_part = expand(
                    coarse_real[piece : piece + 1],
                    coarse_imag[piece : piece + 1],
                    fine_real,
                    fine_imag,
                )
                out_rows[s * facets + a, here, re] = real_part.astype(BF16)
                out_rows[s * facets + a, here, im] = imag_part.astype(BF16)


def strip_tables(meta, sky, steps, geometry):
    count, (rows, columns) = len(steps), sky.shape
    facets = rows // FR
    return pl.pallas_call(
        functools.partial(tables_kernel, steps, geometry),
        in_specs=[SMEM],
        out_specs=[VMEM] * 2,
        out_shape=[
            jax.ShapeDtypeStruct((columns, 2 * count * K), BF16),
            jax.ShapeDtypeStruct((count * facets, FR, 2 * K), BF16),
        ],
        scratch_shapes=[
            pltpu.VMEM((count, columns // STEP, 2 * K), F32),
            pltpu.VMEM((STEP, 2 * K), F32),
        ],
        cost_estimate=pl.CostEstimate(flops=1 << 33, bytes_accessed=1 << 24, transcendentals=0),
        compiler_params=pltpu.CompilerParams(vmem_limit_bytes=16 << 20),
        name="strip_tables",
    )(meta)


def blocks_kernel(at, sky, cols, rows, out):
    facets = sky.shape[0] // FR
    strips = jnp.dot(
        sky[...], cols[:, 2 * at * K : 2 * (at + 1) * K], preferred_element_type=F32
    ).astype(BF16)
    for a in range(facets):
        product = lax.dot_general(
            strips[a * FR : (a + 1) * FR, :],
            rows[at * facets + a],
            (((0,), (0,)), ((), ())),
            preferred_element_type=F32,
        )
        re, im = parts_of(a)
        out[:, re] = (product[:K, :K] - product[K:, K:]).astype(BF16)
        out[:, im] = (product[:K, K:] + product[K:, :K]).astype(BF16)


def facet_blocks(sky, tables, at):
    rows, columns = sky.shape
    return pl.pallas_call(
        functools.partial(blocks_kernel, at),
        in_specs=[VMEM] * 3,
        out_specs=VMEM,
        out_shape=jax.ShapeDtypeStruct((K, 2 * rows // FR * K), BF16),
        cost_estimate=pl.CostEstimate(
            flops=4 * rows * columns * K, bytes_accessed=2 * rows * columns, transcendentals=0
        ),
        compiler_params=pltpu.CompilerParams(vmem_limit_bytes=28 << 20),
        name="facet_blocks",
    )(sky, *tables)


def col_table_kernel(geometry, factor, place, after, out):
    sky_cells, copies, sources = geometry
    planes = len(sources) * copies
    period = 2 * planes
    at_y = place[1]
    plane, core = at_y // 2, at_y % 2
    own = plane // copies
    gap = core * HALF + iota((HALF, K), 0) - SUB // K * iota((HALF, K), 1)
    size = amplitude(gap) * factor
    real_part, imag_part = wave(gap * middle_of(0, sky_cells), sky_cells)
    folded = (HALF // period, period, K)
    real_part = (size * real_part).reshape(folded)
    imag_part = (size * imag_part).reshape(folded)
    steps = gap[:period]
    at = 0
    for other in range(2):
        for step in sources:
            for copy_step in range(copies):
                source = (own ^ step) * copies + (plane % copies ^ copy_step)
                turned = wave(steps * (2 * source + (core + other) % 2), period)
                both = expand(real_part, imag_part, turned[0][None], turned[1][None])
                out[at, :HALF, :] = both[0].reshape(HALF, K).astype(BF16)
                out[at, HALF:, :] = both[1].reshape(HALF, K).astype(BF16)
                at += 1


def row_table_kernel(geometry, place, after, out):
    sky_cells, facets, rows_axis = geometry
    period = facets * rows_axis
    gap = iota((K, SUB), 1) - SUB // K * iota((K, SUB), 0)
    size = amplitude(gap)
    real_part, imag_part = wave(gap * middle_of(0, sky_cells), sky_cells)
    folded = (K // period, period, SUB)
    real_part = (size * real_part).reshape(folded)
    imag_part = (size * imag_part).reshape(folded)
    steps = gap[:period]
    for source in range(period):
        step, a = source // facets, source % facets
        facet_row = (place[0] ^ step) * facets + a
        turned = wave(steps * facet_row, period)
        both = expand(real_part, imag_part, turned[0][None], turned[1][None])
        out[source, :, :SUB] = both[0].reshape(K, SUB).astype(BF16)
        out[source, :, SUB:] = both[1].reshape(K, SUB).astype(BF16)


def columns_kernel(count, facets, table, *refs):
    blocks, out = refs[:count], refs[count]
    total = None
    for pair in range(0, count, 2):
        stacked = jnp.concatenate([block[...] for block in blocks[pair : pair + 2]], axis=0)
        turned = jnp.concatenate([table[at] for at in range(pair, min(pair + 2, count))], axis=1)
        part = jnp.dot(turned, stacked, preferred_element_type=F32)
        total = part if total is None else total + part
    for a in range(facets):
        re, im = parts_of(a)
        out[:HALF, a * K : (a + 1) * K] = (total[:HALF, re] - total[HALF:, im]).astype(BF16)
        out[HALF:, a * K : (a + 1) * K] = (total[:HALF, im] + total[HALF:, re]).astype(BF16)


def column_sums(table, blocks):
    facets = blocks[0].shape[1] // (2 * K)
    return pl.pallas_call(
        functools.partial(columns_kernel, len(blocks), facets),
        out_shape=jax.ShapeDtypeStruct((2 * HALF, facets * K), BF16),
        cost_estimate=pl.CostEstimate(
            flops=8 * HALF * len(blocks) * facets * K * K, bytes_accessed=1 << 21, transcendentals=0
        ),
        compiler_params=pltpu.CompilerParams(vmem_limit_bytes=20 << 20),
        name="column_sums",
    )(table, *blocks)


def taps_of(first, kernel, shape):
    row = iota(shape, 0)
    tap = (row - first) & (W - 1)
    value = jnp.zeros(shape, F32)
    for e in range(W):
        value = jnp.where(tap == e, kernel[e : e + 1, :], value)
    return value, (first - row + (W - 1)) >> 3


def query_kernel(vis_cells, row_kernel, col_kernel, after, out):
    count = vis_cells.shape[1]
    out[:, :count] = row_kernel[...]
    out[:, count : 2 * count] = col_kernel[...].astype(BF16)
    cells = (vis_cells[...] - MIDDLE).astype(F32)
    quarters = [
        cells[axis : axis + 1, at * count // 4 : (at + 1) * count // 4]
        for axis in range(2)
        for at in range(4)
    ]
    out[:, 2 * count :] = jnp.concatenate(quarters, axis=0).astype(BF16)


def row_sums(sums, table):
    total = None
    facets = sums[0].shape[1] // K
    for source, part in enumerate(sums):
        turned = jnp.concatenate(
            [table[at] for at in range(source * facets, (source + 1) * facets)], axis=0
        )
        part = jnp.dot(part[...], turned, preferred_element_type=F32)
        total = part if total is None else total + part
    return total


def partial_kernel(table, *refs):
    refs[-1][...] = row_sums(refs[:-1], table)


def degrid_kernel(geometry, place, readers, table, partial, last, queries_own, queries_other, *refs):
    cols_axis, copies = geometry
    outs, subgrid = refs[:2], refs[2]
    at_x, at_y = place[0], place[1]
    plane, core = at_y // 2, at_y % 2
    own = plane // copies
    facets = last.shape[1] // K
    total = partial[...] + row_sums([last], table[table.shape[0] - facets :])
    subgrid[:HALF, :] = (total[:HALF, :SUB] - total[HALF:, SUB:]).astype(BF16)
    subgrid[HALF:, :] = (total[:HALF, SUB:] + total[HALF:, :SUB]).astype(BF16)
    planes = queries_own.shape[0]
    count = outs[0].shape[2]
    for other, (queries, out) in enumerate(zip((queries_own, queries_other), outs)):

        def slot_turn(slot, carry):
            source = plane ^ slot
            reader = at_x * cols_axis + 2 * source + (core + other) % 2
            active = (readers[reader] == own) & (source % copies == plane % copies)

            @pl.when(jnp.logical_not(active))
            def _():
                out[slot] = jnp.zeros(out.shape[1:], F32)

            @pl.when(active)
            def _():
                values = queries[slot].astype(F32)
                cells = values[:, 2 * count :].astype(jnp.int32) + MIDDLE
                u, w = [
                    jnp.concatenate([cells[4 * axis + at : 4 * axis + at + 1] for at in range(4)], axis=1)
                    for axis in range(2)
                ]
                row_value, row_group = taps_of(u, values[:, :count], (W, count))
                groups = iota((SUB // W, W, count), 0)
                weights = jnp.where(groups == row_group[None], row_value[None], 0.0)
                weights = weights.reshape(SUB, count).astype(BF16)
                spread = jnp.dot(subgrid[...], weights, preferred_element_type=F32)
                spread = spread.reshape(2, HALF // W, W, count)
                col_value, col_group = taps_of(w, values[:, count : 2 * count], (W, count))
                groups = iota((HALF // W, W, count), 0)
                hit = groups == (col_group - core * (HALF // W))[None]
                for p in range(2):
                    picked = jnp.sum(jnp.where(hit, spread[p], 0.0), axis=0)
                    out[slot, p : p + 1, :] = jnp.sum(picked * col_value, axis=0, keepdims=True)

            return carry

        lax.fori_loop(0, planes, slot_turn, 0)


def degrid(place, readers, table, partial, last, queries, others, geometry):
    planes, _, width = queries.shape
    result = jax.ShapeDtypeStruct((planes, 2, width * 4 // 9), F32)
    return pl.pallas_call(
        functools.partial(degrid_kernel, geometry),
        in_specs=[SMEM, SMEM] + [VMEM] * 5,
        out_specs=[VMEM, VMEM],
        out_shape=[result, result],
        scratch_shapes=[pltpu.VMEM((2 * HALF, SUB), BF16)],
        cost_estimate=pl.CostEstimate(flops=1 << 33, bytes_accessed=1 << 22, transcendentals=0),
        compiler_params=pltpu.CompilerParams(vmem_limit_bytes=24 << 20),
        name="degrid",
    )(place, readers, table, partial, last, queries, others)


def local(sky, sub_off, readers, vis_cells, row_kernel, col_kernel):
    rows_axis = lax.axis_size("fx")
    cols_axis = lax.axis_size("fy")
    planes = cols_axis // 2
    copies = planes // NSUB
    facets = sky.shape[0] // FR
    sky_cells = FACET * cols_axis
    facet_rows = facets * rows_axis
    row_spacing = sky_cells // facet_rows
    factor = 1.0 / math.sqrt(facet_rows * cols_axis)
    assert planes == copies * NSUB and not any(
        size & (size - 1) for size in (sky_cells, rows_axis, copies)
    )
    place = jnp.stack([lax.axis_index("fx"), lax.axis_index("fy")]).astype(jnp.int32)
    meta = jnp.concatenate([place, sub_off.reshape(-1)])

    def plane_shift(group_step, copy_step):
        moved = []
        for z in range(planes):
            to = (z // copies ^ group_step) * copies + (z % copies ^ copy_step)
            moved += [(2 * z + c, 2 * to + c) for c in range(2)]
        return moved

    swap = [(i, i ^ 1) for i in range(cols_axis)]

    steps = [*range(2, NSUB), 1, 0]
    blocks = []
    for group in (steps[:-1], steps[-1:]):
        tables = strip_tables(
            meta, sky, group, (sky_cells, row_spacing, copies)
        )
        for at, step in enumerate(group):
            block = facet_blocks(sky, tables, at)
            for copy_step in range(copies):
                moved = block
                if step or copy_step:
                    moved = lax.ppermute(block, "fy", plane_shift(step, copy_step))
                blocks.append(moved)

    col_table = pl.pallas_call(
        functools.partial(col_table_kernel, (sky_cells, copies, steps), factor),
        in_specs=[SMEM, ANY],
        out_specs=VMEM,
        out_shape=jax.ShapeDtypeStruct((2 * len(blocks), 2 * HALF, K), BF16),
        cost_estimate=pl.CostEstimate(flops=1 << 22, bytes_accessed=1 << 20, transcendentals=1 << 20),
        compiler_params=pltpu.CompilerParams(vmem_limit_bytes=20 << 20),
        name="col_table",
    )(place, block)
    query = pl.pallas_call(
        query_kernel,
        in_specs=[VMEM, VMEM, VMEM, ANY],
        out_specs=VMEM,
        out_shape=jax.ShapeDtypeStruct((W, vis_cells.shape[1] * 9 // 4), BF16),
        compiler_params=pltpu.CompilerParams(vmem_limit_bytes=20 << 20),
        name="query",
    )(vis_cells, row_kernel, col_kernel, block)
    *blocks[: 2 * copies], _ = lax.optimization_barrier((*blocks[: 2 * copies], col_table))
    blocks += [lax.ppermute(block, "fy", swap) for block in blocks]
    sums = [column_sums(col_table, blocks)]

    for step in range(1, rows_axis):
        sums.append(lax.ppermute(sums[0], "fx", [(i, i ^ step) for i in range(rows_axis)]))
    row_table = pl.pallas_call(
        functools.partial(row_table_kernel, (sky_cells, facets, rows_axis)),
        in_specs=[SMEM, ANY],
        out_specs=VMEM,
        out_shape=jax.ShapeDtypeStruct((facet_rows, K, 2 * SUB), BF16),
        cost_estimate=pl.CostEstimate(
            flops=1 << 23, bytes_accessed=1 << 21, transcendentals=1 << 21
        ),
        compiler_params=pltpu.CompilerParams(vmem_limit_bytes=20 << 20),
        name="row_table",
    )(place, sums[0])

    moved, _ = lax.optimization_barrier((query, sums[0]))
    queries = [query]
    for step in range(1, planes):
        ring = [(i, i ^ 2 * step) for i in range(cols_axis)]
        queries.append(lax.ppermute(moved, "fy", ring))
    queries = jnp.stack(queries)
    others = lax.ppermute(queries, "fy", swap)
    partial = pl.pallas_call(
        partial_kernel,
        in_specs=[VMEM] * rows_axis,
        out_specs=VMEM,
        out_shape=jax.ShapeDtypeStruct((2 * HALF, 2 * SUB), F32),
        cost_estimate=pl.CostEstimate(
            flops=8 * HALF * SUB * facet_rows * K, bytes_accessed=1 << 22, transcendentals=0
        ),
        compiler_params=pltpu.CompilerParams(vmem_limit_bytes=20 << 20),
        name="partial_rows",
    )(row_table, *sums[:-1])
    results, others = degrid(
        place, readers, row_table, partial, sums[-1], queries, others, (cols_axis, copies)
    )

    both = results + lax.ppermute(others, "fy", swap)
    vis = both[0]
    for step in range(1, planes):
        ring = [(i, i ^ 2 * step) for i in range(cols_axis)]
        vis = vis + lax.ppermute(both[step], "fy", ring)
    return vis


def solution(mesh):
    return jax.shard_map(
        local,
        mesh=mesh,
        in_specs=(
            P("fx", "fy"),
            P(),
            P(),
            P(None, ("fx", "fy")),
            P(None, ("fx", "fy")),
            P(None, ("fx", "fy")),
        ),
        out_specs=P(None, ("fx", "fy")),
        check_vma=False,
    )
```

```python
import functools
import math

import jax
import jax.numpy as jnp
from jax import lax
from jax.experimental import pallas as pl
from jax.experimental.pallas import tpu as pltpu
from jax.sharding import PartitionSpec as P


FACET = 4096
SUB = 512
K = 128
FR = 512
NSUB = 4
W = 8
STEP = 64
GROUP = 8
TILE = 16
MIDDLE = (SUB - W) // 2
HALF = SUB // 2
F32 = jnp.float32
BF16 = jnp.bfloat16
SMEM = pl.BlockSpec(memory_space=pltpu.SMEM)
VMEM = pl.BlockSpec(memory_space=pltpu.VMEM)
ANY = pl.BlockSpec(memory_space=pl.ANY)


def wave(turns, period):
    bits = period.bit_length() - 1
    phase = turns & (period - 1)
    quarter = (phase + period // 8) >> (bits - 2)
    theta = (phase - (quarter << (bits - 2))).astype(F32) * (2.0 * math.pi / period)
    square = theta * theta
    sine = theta * (
        1.0
        + square
        * (-1.0 / 6 + square * (1.0 / 120 + square * (-1.0 / 5040 + square * (1.0 / 362880))))
    )
    cosine = 1.0 + square * (
        -0.5
        + square
        * (1.0 / 24 + square * (-1.0 / 720 + square * (1.0 / 40320 - square * (1.0 / 3628800))))
    )
    odd = (quarter & 1) == 1
    real_part = jnp.where(odd, sine, cosine)
    imag_part = jnp.where(odd, cosine, sine)
    real_part = jnp.where(((quarter + 1) & 2) == 2, -real_part, real_part)
    imag_part = jnp.where((quarter & 2) == 2, -imag_part, imag_part)
    return real_part, imag_part


def turn(first, second, sky_cells, scale=1.0):
    real_part, imag_part = wave(first * second, sky_cells)
    return real_part * scale, imag_part * -scale


def amplitude(gap):
    top = wave(gap, 2 * SUB // K)[1]
    below = wave(gap, 2 * SUB)[1]
    return jnp.where(gap == 0, 1.0, top / (K * jnp.where(gap == 0, 1.0, below)))


def middle_of(start, sky_cells):
    return start + (K - 1) * (sky_cells // (2 * SUB))


def iota(shape, dimension):
    return lax.broadcasted_iota(jnp.int32, shape, dimension)


def expand(coarse_real, coarse_imag, fine_real, fine_imag):
    return (
        coarse_real * fine_real - coarse_imag * fine_imag,
        coarse_real * fine_imag + coarse_imag * fine_real,
    )


def parts_of(index):
    return slice(2 * index * K, (2 * index + 1) * K), slice((2 * index + 1) * K, (2 * index + 2) * K)


def tables_kernel(steps, geometry, meta, out_cols, out_rows, coarse_col, fine_col):
    sky_cells, row_spacing, copies = geometry
    count, columns = len(steps), out_cols.shape[0]
    facets = out_rows.shape[0] // count
    at_x, at_y = meta[0], meta[1]
    own = at_y // 2 // copies
    lane, row = iota((STEP, K), 1), iota((STEP, K), 0)
    re, im = parts_of(0)
    for s, step in enumerate(steps):
        chosen = own ^ step
        out_re, out_im = parts_of(s)
        frequency = meta[2 + NSUB + chosen] + SUB // K * lane
        coarse_col[s, :, re], coarse_col[s, :, im] = turn(
            frequency, at_y * FACET + STEP * row, sky_cells, 1.0 / math.sqrt(FACET)
        )
        fine_col[:, re], fine_col[:, im] = turn(frequency, row, sky_cells)

        def table_turn(group, carry):
            coarse = coarse_col[s, pl.ds(pl.multiple_of(group * GROUP, GROUP), GROUP), :]
            for tile in range(0, STEP, TILE):
                fine_real, fine_imag = fine_col[tile : tile + TILE, re], fine_col[tile : tile + TILE, im]
                for piece in range(GROUP):
                    here = pl.ds(pl.multiple_of((group * GROUP + piece) * STEP + tile, TILE), TILE)
                    real_part, imag_part = expand(
                        coarse[piece : piece + 1, re],
                        coarse[piece : piece + 1, im],
                        fine_real,
                        fine_imag,
                    )
                    out_cols[here, out_re] = real_part.astype(BF16)
                    out_cols[here, out_im] = imag_part.astype(BF16)
            return carry

        lax.fori_loop(0, columns // (STEP * GROUP), table_turn, 0)
        frequency = meta[2 + chosen] + SUB // K * lane
        fine_real, fine_imag = turn(frequency, row, sky_cells)
        pieces = FR // STEP
        for a in range(facets):
            row_start = (at_x * facets + a) * row_spacing
            coarse_real, coarse_imag = turn(
                frequency[:pieces], row_start + STEP * row[:pieces], sky_cells, 1.0 / math.sqrt(FR)
            )
            for piece in range(pieces):
                here = slice(piece * STEP, (piece + 1) * STEP)
                real_part, imag_part = expand(
                    coarse_real[piece : piece + 1],
                    coarse_imag[piece : piece + 1],
                    fine_real,
                    fine_imag,
                )
                out_rows[s * facets + a, here, re] = real_part.astype(BF16)
                out_rows[s * facets + a, here, im] = imag_part.astype(BF16)


def strip_tables(meta, sky, steps, geometry):
    count, (rows, columns) = len(steps), sky.shape
    facets = rows // FR
    return pl.pallas_call(
        functools.partial(tables_kernel, steps, geometry),
        in_specs=[SMEM],
        out_specs=[VMEM] * 2,
        out_shape=[
            jax.ShapeDtypeStruct((columns, 2 * count * K), BF16),
            jax.ShapeDtypeStruct((count * facets, FR, 2 * K), BF16),
        ],
        scratch_shapes=[
            pltpu.VMEM((count, columns // STEP, 2 * K), F32),
            pltpu.VMEM((STEP, 2 * K), F32),
        ],
        cost_estimate=pl.CostEstimate(flops=1 << 33, bytes_accessed=1 << 24, transcendentals=0),
        compiler_params=pltpu.CompilerParams(vmem_limit_bytes=16 << 20),
        name="strip_tables",
    )(meta)


def blocks_kernel(at, sky, cols, rows, out):
    facets = sky.shape[0] // FR
    strips = jnp.dot(
        sky[...], cols[:, 2 * at * K : 2 * (at + 1) * K], preferred_element_type=F32
    ).astype(BF16)
    for a in range(facets):
        product = lax.dot_general(
            strips[a * FR : (a + 1) * FR, :],
            rows[at * facets + a],
            (((0,), (0,)), ((), ())),
            preferred_element_type=F32,
        )
        re, im = parts_of(a)
        out[:, re] = (product[:K, :K] - product[K:, K:]).astype(BF16)
        out[:, im] = (product[:K, K:] + product[K:, :K]).astype(BF16)


def facet_blocks(sky, tables, at):
    rows, columns = sky.shape
    return pl.pallas_call(
        functools.partial(blocks_kernel, at),
        in_specs=[VMEM] * 3,
        out_specs=VMEM,
        out_shape=jax.ShapeDtypeStruct((K, 2 * rows // FR * K), BF16),
        cost_estimate=pl.CostEstimate(
            flops=4 * rows * columns * K, bytes_accessed=2 * rows * columns, transcendentals=0
        ),
        compiler_params=pltpu.CompilerParams(vmem_limit_bytes=28 << 20),
        name="facet_blocks",
    )(sky, *tables)


def col_table_kernel(geometry, factor, place, after, out):
    sky_cells, copies, sources = geometry
    planes = len(sources) * copies
    period = 2 * planes
    at_y = place[1]
    plane, core = at_y // 2, at_y % 2
    own = plane // copies
    gap = core * HALF + iota((HALF, K), 0) - SUB // K * iota((HALF, K), 1)
    size = amplitude(gap) * factor
    real_part, imag_part = wave(gap * middle_of(0, sky_cells), sky_cells)
    folded = (HALF // period, period, K)
    real_part = (size * real_part).reshape(folded)
    imag_part = (size * imag_part).reshape(folded)
    steps = gap[:period]
    at = 0
    for other in range(2):
        for step in sources:
            for copy_step in range(copies):
                source = (own ^ step) * copies + (plane % copies ^ copy_step)
                turned = wave(steps * (2 * source + (core + other) % 2), period)
                both = expand(real_part, imag_part, turned[0][None], turned[1][None])
                out[at, :HALF, :] = both[0].reshape(HALF, K).astype(BF16)
                out[at, HALF:, :] = both[1].reshape(HALF, K).astype(BF16)
                at += 1


def row_table_kernel(geometry, place, after, out):
    sky_cells, facets, rows_axis = geometry
    period = facets * rows_axis
    gap = iota((K, SUB), 1) - SUB // K * iota((K, SUB), 0)
    size = amplitude(gap)
    real_part, imag_part = wave(gap * middle_of(0, sky_cells), sky_cells)
    folded = (K // period, period, SUB)
    real_part = (size * real_part).reshape(folded)
    imag_part = (size * imag_part).reshape(folded)
    steps = gap[:period]
    for source in range(period):
        step, a = source // facets, source % facets
        facet_row = (place[0] ^ step) * facets + a
        turned = wave(steps * facet_row, period)
        both = expand(real_part, imag_part, turned[0][None], turned[1][None])
        out[source, :, :SUB] = both[0].reshape(K, SUB).astype(BF16)
        out[source, :, SUB:] = both[1].reshape(K, SUB).astype(BF16)


def columns_kernel(count, facets, table, *refs):
    blocks, out = refs[:count], refs[count]
    total = None
    for pair in range(0, count, 2):
        stacked = jnp.concatenate([block[...] for block in blocks[pair : pair + 2]], axis=0)
        turned = jnp.concatenate([table[at] for at in range(pair, min(pair + 2, count))], axis=1)
        part = jnp.dot(turned, stacked, preferred_element_type=F32)
        total = part if total is None else total + part
    for a in range(facets):
        re, im = parts_of(a)
        out[:HALF, a * K : (a + 1) * K] = (total[:HALF, re] - total[HALF:, im]).astype(BF16)
        out[HALF:, a * K : (a + 1) * K] = (total[:HALF, im] + total[HALF:, re]).astype(BF16)


def column_sums(table, blocks):
    facets = blocks[0].shape[1] // (2 * K)
    return pl.pallas_call(
        functools.partial(columns_kernel, len(blocks), facets),
        out_shape=jax.ShapeDtypeStruct((2 * HALF, facets * K), BF16),
        cost_estimate=pl.CostEstimate(
            flops=8 * HALF * len(blocks) * facets * K * K, bytes_accessed=1 << 21, transcendentals=0
        ),
        compiler_params=pltpu.CompilerParams(vmem_limit_bytes=20 << 20),
        name="column_sums",
    )(table, *blocks)


def taps_of(first, kernel, shape):
    row = iota(shape, 0)
    tap = (row - first) & (W - 1)
    value = jnp.zeros(shape, F32)
    for e in range(W):
        value = jnp.where(tap == e, kernel[e : e + 1, :], value)
    return value, (first - row + (W - 1)) >> 3


def query_kernel(vis_cells, row_kernel, col_kernel, after, out):
    count = vis_cells.shape[1]
    out[:, :count] = row_kernel[...]
    out[:, count : 2 * count] = col_kernel[...].astype(BF16)
    cells = (vis_cells[...] - MIDDLE).astype(F32)
    quarters = [
        cells[axis : axis + 1, at * count // 4 : (at + 1) * count // 4]
        for axis in range(2)
        for at in range(4)
    ]
    out[:, 2 * count :] = jnp.concatenate(quarters, axis=0).astype(BF16)


def row_sums(sums, table):
    total = None
    facets = sums[0].shape[1] // K
    for source, part in enumerate(sums):
        turned = jnp.concatenate(
            [table[at] for at in range(source * facets, (source + 1) * facets)], axis=0
        )
        part = jnp.dot(part[...], turned, preferred_element_type=F32)
        total = part if total is None else total + part
    return total


def partial_kernel(table, *refs):
    refs[-1][...] = row_sums(refs[:-1], table)


def degrid_kernel(geometry, place, readers, table, partial, last, queries_own, queries_other, *refs):
    cols_axis, copies = geometry
    outs, subgrid = refs[:2], refs[2]
    at_x, at_y = place[0], place[1]
    plane, core = at_y // 2, at_y % 2
    own = plane // copies
    facets = last.shape[1] // K
    total = partial[...] + row_sums([last], table[table.shape[0] - facets :])
    subgrid[:HALF, :] = (total[:HALF, :SUB] - total[HALF:, SUB:]).astype(BF16)
    subgrid[HALF:, :] = (total[:HALF, SUB:] + total[HALF:, :SUB]).astype(BF16)
    planes = queries_own.shape[0]
    count = outs[0].shape[2]
    for other, (queries, out) in enumerate(zip((queries_own, queries_other), outs)):

        def slot_turn(slot, carry):
            source = plane ^ slot
            reader = at_x * cols_axis + 2 * source + (core + other) % 2
            active = (readers[reader] == own) & (source % copies == plane % copies)

            @pl.when(jnp.logical_not(active))
            def _():
                out[slot] = jnp.zeros(out.shape[1:], F32)

            @pl.when(active)
            def _():
                values = queries[slot].astype(F32)
                cells = values[:, 2 * count :].astype(jnp.int32) + MIDDLE
                u, w = [
                    jnp.concatenate([cells[4 * axis + at : 4 * axis + at + 1] for at in range(4)], axis=1)
                    for axis in range(2)
                ]
                row_value, row_group = taps_of(u, values[:, :count], (W, count))
                groups = iota((SUB // W, W, count), 0)
                weights = jnp.where(groups == row_group[None], row_value[None], 0.0)
                weights = weights.reshape(SUB, count).astype(BF16)
                spread = jnp.dot(subgrid[...], weights, preferred_element_type=F32)
                spread = spread.reshape(2, HALF // W, W, count)
                col_value, col_group = taps_of(w, values[:, count : 2 * count], (W, count))
                groups = iota((HALF // W, W, count), 0)
                hit = groups == (col_group - core * (HALF // W))[None]
                for p in range(2):
                    picked = jnp.sum(jnp.where(hit, spread[p], 0.0), axis=0)
                    out[slot, p : p + 1, :] = jnp.sum(picked * col_value, axis=0, keepdims=True)

            return carry

        lax.fori_loop(0, planes, slot_turn, 0)


def degrid(place, readers, table, partial, last, queries, others, geometry):
    planes, _, width = queries.shape
    result = jax.ShapeDtypeStruct((planes, 2, width * 4 // 9), F32)
    return pl.pallas_call(
        functools.partial(degrid_kernel, geometry),
        in_specs=[SMEM, SMEM] + [VMEM] * 5,
        out_specs=[VMEM, VMEM],
        out_shape=[result, result],
        scratch_shapes=[pltpu.VMEM((2 * HALF, SUB), BF16)],
        cost_estimate=pl.CostEstimate(flops=1 << 33, bytes_accessed=1 << 22, transcendentals=0),
        compiler_params=pltpu.CompilerParams(vmem_limit_bytes=24 << 20),
        name="degrid",
    )(place, readers, table, partial, last, queries, others)


def local(sky, sub_off, readers, vis_cells, row_kernel, col_kernel):
    rows_axis = lax.axis_size("fx")
    cols_axis = lax.axis_size("fy")
    planes = cols_axis // 2
    copies = planes // NSUB
    facets = sky.shape[0] // FR
    sky_cells = FACET * cols_axis
    facet_rows = facets * rows_axis
    row_spacing = sky_cells // facet_rows
    factor = 1.0 / math.sqrt(facet_rows * cols_axis)
    assert planes == copies * NSUB and not any(
        size & (size - 1) for size in (sky_cells, rows_axis, copies)
    )
    place = jnp.stack([lax.axis_index("fx"), lax.axis_index("fy")]).astype(jnp.int32)
    meta = jnp.concatenate([place, sub_off.reshape(-1)])

    def plane_shift(group_step, copy_step):
        moved = []
        for z in range(planes):
            to = (z // copies ^ group_step) * copies + (z % copies ^ copy_step)
            moved += [(2 * z + c, 2 * to + c) for c in range(2)]
        return moved

    swap = [(i, i ^ 1) for i in range(cols_axis)]

    steps = [*range(2, NSUB), 1, 0]
    blocks = []
    tables = strip_tables(meta, sky, steps, (sky_cells, row_spacing, copies))
    for at, step in enumerate(steps):
        block = facet_blocks(sky, tables, at)
        for copy_step in range(copies):
            moved = block
            if step or copy_step:
                moved = lax.ppermute(block, "fy", plane_shift(step, copy_step))
            blocks.append(moved)

    col_table = pl.pallas_call(
        functools.partial(col_table_kernel, (sky_cells, copies, steps), factor),
        in_specs=[SMEM, ANY],
        out_specs=VMEM,
        out_shape=jax.ShapeDtypeStruct((2 * len(blocks), 2 * HALF, K), BF16),
        cost_estimate=pl.CostEstimate(flops=1 << 22, bytes_accessed=1 << 20, transcendentals=1 << 20),
        compiler_params=pltpu.CompilerParams(vmem_limit_bytes=20 << 20),
        name="col_table",
    )(place, block)
    query = pl.pallas_call(
        query_kernel,
        in_specs=[VMEM, VMEM, VMEM, ANY],
        out_specs=VMEM,
        out_shape=jax.ShapeDtypeStruct((W, vis_cells.shape[1] * 9 // 4), BF16),
        compiler_params=pltpu.CompilerParams(vmem_limit_bytes=20 << 20),
        name="query",
    )(vis_cells, row_kernel, col_kernel, block)
    *blocks[: 2 * copies], _ = lax.optimization_barrier((*blocks[: 2 * copies], col_table))
    blocks += [lax.ppermute(block, "fy", swap) for block in blocks]
    sums = [column_sums(col_table, blocks)]

    for step in range(1, rows_axis):
        sums.append(lax.ppermute(sums[0], "fx", [(i, i ^ step) for i in range(rows_axis)]))
    row_table = pl.pallas_call(
        functools.partial(row_table_kernel, (sky_cells, facets, rows_axis)),
        in_specs=[SMEM, ANY],
        out_specs=VMEM,
        out_shape=jax.ShapeDtypeStruct((facet_rows, K, 2 * SUB), BF16),
        cost_estimate=pl.CostEstimate(
            flops=1 << 23, bytes_accessed=1 << 21, transcendentals=1 << 21
        ),
        compiler_params=pltpu.CompilerParams(vmem_limit_bytes=20 << 20),
        name="row_table",
    )(place, sums[0])

    moved, _ = lax.optimization_barrier((query, sums[0]))
    queries = [query]
    for step in range(1, planes):
        ring = [(i, i ^ 2 * step) for i in range(cols_axis)]
        queries.append(lax.ppermute(moved, "fy", ring))
    queries = jnp.stack(queries)
    others = lax.ppermute(queries, "fy", swap)
    partial = pl.pallas_call(
        partial_kernel,
        in_specs=[VMEM] * rows_axis,
        out_specs=VMEM,
        out_shape=jax.ShapeDtypeStruct((2 * HALF, 2 * SUB), F32),
        cost_estimate=pl.CostEstimate(
            flops=8 * HALF * SUB * facet_rows * K, bytes_accessed=1 << 22, transcendentals=0
        ),
        compiler_params=pltpu.CompilerParams(vmem_limit_bytes=20 << 20),
        name="partial_rows",
    )(row_table, *sums[:-1])
    results, others = degrid(
        place, readers, row_table, partial, sums[-1], queries, others, (cols_axis, copies)
    )

    both = results + lax.ppermute(others, "fy", swap)
    vis = both[0]
    for step in range(1, planes):
        ring = [(i, i ^ 2 * step) for i in range(cols_axis)]
        vis = vis + lax.ppermute(both[step], "fy", ring)
    return vis


def solution(mesh):
    return jax.shard_map(
        local,
        mesh=mesh,
        in_specs=(
            P("fx", "fy"),
            P(),
            P(),
            P(None, ("fx", "fy")),
            P(None, ("fx", "fy")),
            P(None, ("fx", "fy")),
        ),
        out_specs=P(None, ("fx", "fy")),
        check_vma=False,
    )
```
